32 devices in a mesh: shard: 4 (over y, x), ctx: 2 (over core), tp: 4 (over z).
Axes of the slice: x: 2, y: 2, z: 4, core: 2. Of those that a mesh axis runs over, the one named last changes fastest.
Arguments:
- latents: bfloat16 [4, 2048, 1024], P('shard', 'ctx'), may hold values from -6 to 6
- condition: bfloat16 [4, 1024], P('shard'), may hold values from -6 to 6
- modulation_weight: bfloat16 [1024, 6, 1024], P(('shard', 'ctx'), None, 'tp'), may hold values from -0.1875 to 0.1875
- modulation_bias: bfloat16 [6, 1024], P(None, 'tp'), may hold values from -3 to 3
- heads_weight: bfloat16 [1024, 3, 1024], P(('shard', 'ctx'), None, 'tp'), may hold values from -0.1875 to 0.1875
- heads_bias: bfloat16 [2, 1024], P(None, 'tp'), may hold values from -1.25 to 1.25
- merge_weight: bfloat16 [1024, 1024], P(('shard', 'ctx'), 'tp'), may hold values from -0.75 to 0.75
- merge_bias: bfloat16 [1024], replicated, may hold values from -3 to 3
- expand_weight: bfloat16 [1024, 4096], P(('shard', 'ctx'), 'tp'), may hold values from -0.1875 to 0.1875
- expand_bias: bfloat16 [4096], P('tp'), may hold values from -3 to 3
- reduce_weight: bfloat16 [1024, 4096], P(('shard', 'ctx'), 'tp'), may hold values from -0.09375 to 0.09375
- reduce_bias: bfloat16 [1024], replicated, may hold values from -3 to 3
- cotangent: bfloat16 [4, 2048, 1024], P('shard', 'ctx'), may hold values from -6 to 6
Outputs:
- output: bfloat16 [4, 2048, 1024], P('shard', 'ctx')
- latents_grad: float32 [4, 2048, 1024], P('shard', 'ctx')
- modulation_weight_grad: float32 [1024, 6, 1024], P(('shard', 'ctx'), None, 'tp')
- modulation_bias_grad: float32 [6, 1024], P(None, 'tp')
- heads_weight_grad: float32 [1024, 3, 1024], P(('shard', 'ctx'), None, 'tp')
- heads_bias_grad: float32 [2, 1024], P(None, 'tp')
- merge_weight_grad: float32 [1024, 1024], P(('shard', 'ctx'), 'tp')
- merge_bias_grad: float32 [1024], replicated
- expand_weight_grad: float32 [1024, 4096], P(('shard', 'ctx'), 'tp')
- expand_bias_grad: float32 [4096], P('tp')
- reduce_weight_grad: float32 [1024, 4096], P(('shard', 'ctx'), 'tp')
- reduce_bias_grad: float32 [1024], replicated
The draws below stay inside these ranges and needn't reach their ends.
All inputs are finite; a program needn't handle non-finite values.
Results may differ from the reference program's by a relative error of at most 0.018.
The reference program's roundings to bfloat16 on the way count: a program that leaves them out, or rounds other values in their place, can miss the bound.
Values may be sent and summed in bfloat16 or wider, within the bound.
No kernel may reach another device: no remote copies, remote signals or barrier semaphores. Data moves between devices by JAX's collectives and lax.ppermute only.
A program may use at most 192 MiB of HBM per device.

```python
import jax
import jax.numpy as jnp
from jax import lax

D = 1024
HEADS = 16
FF = 4096
HD = 64
SEQ = 2048
LATENTS = 4


def level_of(rng, shape, pieces, low, largest):
    def one(dim, blocks):
        steps = jax.random.uniform(jax.random.fold_in(jax.random.fold_in(rng, 6), dim), (blocks,), jnp.float32, low / len(pieces), largest / len(pieces))
        return jnp.repeat(jnp.exp(steps), shape[dim] // blocks).reshape((-1,) + (1,) * (len(shape) - dim - 1))

    factor_of = one(*pieces[0])
    for cut in pieces[1:]:
        factor_of = factor_of * one(*cut)
    return factor_of


def gaussian(stream_key, dims, deviation, most, split=(), held_as=jnp.bfloat16):
    array = deviation * jax.random.normal(stream_key, dims, jnp.float32)
    if split:
        array = array * level_of(stream_key, dims, split, -0.22, 0.18)
    return jnp.clip(array, -most, most).astype(held_as)


def setup_inputs(seed: int = 0) -> dict:
    seeds = jax.random.split(jax.random.key(seed), 14)
    latents = gaussian(seeds[0], (LATENTS, SEQ, D), 1.0, 6.0, ((0, 4), (1, 2)))
    condition = gaussian(seeds[1], (LATENTS, D), 1.0, 6.0, ((0, 4),))
    modulation_weight = gaussian(seeds[2], (D, 6, D), D ** -0.5, 0.1875, ((0, 8), (2, 4)))
    modulation_bias = gaussian(seeds[3], (6, D), 0.5, 3.0, ((1, 4),))
    heads_weight = gaussian(seeds[4], (D, 3, D), D ** -0.5, 0.1875, ((0, 8), (2, 4)))
    heads_bias = gaussian(seeds[5], (2, D), 0.2, 1.25, ((1, 4),))
    merge_weight = gaussian(seeds[6], (D, D), (D // 16) ** -0.5, 0.75, ((0, 8), (1, 4)))
    merge_bias = gaussian(seeds[7], (D,), 0.5, 3.0)
    expand_weight = gaussian(seeds[8], (D, FF), D ** -0.5, 0.1875, ((0, 8), (1, 4)))
    expand_bias = gaussian(seeds[9], (FF,), 0.5, 3.0, ((0, 4),))
    reduce_weight = gaussian(seeds[10], (D, FF), FF ** -0.5, 0.09375, ((0, 8), (1, 4)))
    reduce_bias = gaussian(seeds[11], (D,), 0.5, 3.0)
    cotangent = gaussian(seeds[12], (LATENTS, SEQ, D), 1.0, 6.0, ((0, 4), (1, 2)))
    return dict(latents=latents, condition=condition, modulation_weight=modulation_weight, modulation_bias=modulation_bias, heads_weight=heads_weight, heads_bias=heads_bias, merge_weight=merge_weight, merge_bias=merge_bias, expand_weight=expand_weight, expand_bias=expand_bias, reduce_weight=reduce_weight, reduce_bias=reduce_bias, cotangent=cotangent)


@jax.custom_vjp
def low(v):
    return lax.optimization_barrier(v.astype(jnp.bfloat16)).astype(jnp.float32)

@jax.custom_vjp
def low_back(v):
    return v

def low_keep(v):
    return (low(v), None)

def low_pass(kept, grad):
    return (grad,)

def back_keep(v):
    return (v, None)

def back_low(kept, grad):
    return (low(grad),)
low.defvjp(low_keep, low_pass)
low_back.defvjp(back_keep, back_low)

def modulate(values, offset, scaling):
    centre = values - lax.optimization_barrier(jnp.mean(values, axis=-1, keepdims=True))
    variance = lax.optimization_barrier(jnp.mean(centre * centre, axis=-1, keepdims=True))
    normed = centre * lax.rsqrt(variance + 1e-06)
    return normed * (1.0 + scaling) + offset

def block(latent, condition_row, modulation_weight, modulation_bias, heads_weight, heads_bias, merge_weight, merge_bias, expand_weight, expand_bias, reduce_weight, reduce_bias):
    highest = lax.Precision.HIGHEST
    silu_condition = low(jax.nn.silu(condition_row))
    modulation = jnp.einsum('d,dkf->kf', silu_condition, modulation_weight, precision=highest) + modulation_bias
    offset_one = modulation[0]
    scaling_one = modulation[1]
    gate_one = modulation[2]
    offset_two = modulation[3]
    scaling_two = modulation[4]
    gate_two = modulation[5]
    normed_one = low(modulate(latent, offset_one, scaling_one))
    projected = jnp.einsum('sd,dkf->skf', normed_one, heads_weight, precision=highest)
    zeros_row = jnp.zeros_like(heads_bias[0])
    projected = low(low_back(projected + jnp.stack([heads_bias[0], zeros_row, heads_bias[1]])))
    queries = projected[:, 0].reshape(SEQ, HEADS, HD)
    key_rows = projected[:, 1].reshape(SEQ, HEADS, HD)
    value_rows = projected[:, 2].reshape(SEQ, HEADS, HD)
    scores = low_back(jnp.einsum('qhd,khd->hqk', queries, key_rows, precision=highest) * HD ** (-0.5))
    attention = jax.nn.softmax(scores, axis=-1)
    blended_heads = jnp.einsum('hqk,khd->qhd', low(attention), value_rows, precision=highest).reshape(SEQ, D)
    blended_heads = low(low_back(blended_heads))
    branch_one = low_back(jnp.einsum('sf,df->sd', blended_heads, merge_weight, precision=highest) + merge_bias)
    middle = latent + gate_one * branch_one
    normed_two = low(modulate(middle, offset_two, scaling_two))
    hidden = low_back(jnp.dot(normed_two, expand_weight, precision=highest) + expand_bias)
    activated = low(jax.nn.gelu(hidden, approximate=True))
    branch_two = low_back(jnp.einsum('sh,dh->sd', activated, reduce_weight, precision=highest) + reduce_bias)
    return middle + gate_two * branch_two

def reference(latents, condition, modulation_weight, modulation_bias, heads_weight, heads_bias, merge_weight, merge_bias, expand_weight, expand_bias, reduce_weight, reduce_bias, cotangent):
    params = tuple((weight.astype(jnp.float32) for weight in (modulation_weight, modulation_bias, heads_weight, heads_bias, merge_weight, merge_bias, expand_weight, expand_bias, reduce_weight, reduce_bias)))

    def one_latent(totals, inputs):
        latent, condition_row, cotangent_row = inputs

        def forward(latent_in, *weights):
            return block(latent_in, condition_row.astype(jnp.float32), *weights)
        result, pullback = jax.vjp(forward, latent.astype(jnp.float32), *params)
        gradients = pullback(cotangent_row.astype(jnp.float32))
        totals = tuple((running + addend for running, addend in zip(totals, gradients[1:])))
        return (totals, (result.astype(jnp.bfloat16), gradients[0]))
    starts = tuple((jnp.zeros(weight.shape, jnp.float32) for weight in params))
    totals, (output, latents_grad) = lax.scan(one_latent, starts, (latents, condition, cotangent))
    return (output, latents_grad, totals[0], totals[1], totals[2], totals[3], totals[4], totals[5], totals[6], totals[7], totals[8], totals[9])
```

```python
import functools

import jax
import jax.numpy as jnp
from jax import lax
from jax.experimental import pallas as pl
from jax.experimental.pallas import tpu as pltpu
from jax.sharding import PartitionSpec as P

HD = 64


def shift(values, axis, size, offset):
    return lax.ppermute(values, axis, [(i, (i + offset) % size) for i in range(size)])


def rotated(values, axis, size):
    return [values] + [shift(values, axis, size, k) for k in range(1, size)]


def add_all(values, axis, size):
    if size & (size - 1):
        return lax.psum(values, axis)
    step = 1
    while step < size:
        values = values + lax.ppermute(values, axis, [(i, i ^ step) for i in range(size)])
        step *= 2
    return values


def gather_small(values, axis, size):
    if size > 8:
        return lax.all_gather(values, axis)
    pieces = rotated(values, axis, size)
    here = lax.axis_index(axis)
    rows = []
    for j in range(size):
        row = pieces[0]
        for k in range(1, size):
            row = jnp.where((here - j) % size == k, pieces[k], row)
        rows.append(row)
    return jnp.stack(rows)


def scatter_small(values, axis, size):
    if size > 8:
        return lax.psum_scatter(values, axis)
    here = lax.axis_index(axis)

    def piece(k):
        return lax.dynamic_index_in_dim(values, (here + k) % size, 0, keepdims=False)

    total = piece(0)
    for k in range(1, size):
        total = total + shift(piece(k), axis, size, k)
    return total


def block_of(values, index, count):
    return lax.dynamic_slice_in_dim(values, index * count, count, 0)


def reduce_rows(values, axis, size):
    here = lax.axis_index(axis)
    count = values.shape[0] // size
    total = block_of(values, here, count).astype(jnp.float32)
    for k in range(1, size):
        sent = block_of(values, (here + k) % size, count)
        total = total + shift(sent, axis, size, k).astype(jnp.float32)
    return total


def place_rows(pieces, first, step, size):
    count = pieces[0].shape[0]
    whole = jnp.zeros((size * count,) + pieces[0].shape[1:], pieces[0].dtype)
    for k, piece in enumerate(pieces):
        whole = lax.dynamic_update_slice_in_dim(whole, piece, ((first + step * k) % size) * count, 0)
    return whole


def gather_rows(values, axis, size):
    return place_rows(rotated(values, axis, size), lax.axis_index(axis), -1, size)


def normalise(values):
    centre = values - jnp.mean(values, axis=-1, keepdims=True)
    variance = jnp.mean(centre * centre, axis=-1, keepdims=True)
    scale = lax.rsqrt(variance + 1e-06)
    return centre * scale, scale


def normalise_back(grad, normed, scale):
    inner = grad - jnp.mean(grad, axis=-1, keepdims=True)
    return scale * (inner - normed * jnp.mean(grad * normed, axis=-1, keepdims=True))


def smooth_gate(values):
    return jax.nn.gelu(values, approximate=True)


def product(text, left, right):
    return jnp.einsum(text, left, right, preferred_element_type=jnp.float32)


def head_lanes(shape, head):
    lane = lax.broadcasted_iota(jnp.int32, shape, 1)
    return (lane >= head * HD) & (lane < (head + 1) * HD)


def dot(left, right, dims):
    return lax.dot_general(left, right, (dims, ((), ())), preferred_element_type=jnp.float32)


ROWS = ((1,), (1,))
PLAIN = ((1,), (0,))


def attend_kernel(query, key_a, key_b, value_a, value_b, mixed, mixed_wide, log_total):
    queries = query[...] * jnp.asarray(HD ** (-0.5), jnp.bfloat16)
    gathered = jnp.zeros(mixed_wide.shape, jnp.float32)
    for head in range(queries.shape[1] // HD):
        lanes = head_lanes(queries.shape, head)
        own = jnp.where(lanes, queries, jnp.zeros_like(queries))
        score_a = dot(own, key_a[...], ROWS)
        score_b = dot(own, key_b[...], ROWS)
        top = jnp.maximum(
            jnp.max(score_a, axis=1, keepdims=True), jnp.max(score_b, axis=1, keepdims=True)
        )
        exp_a = jnp.exp(score_a - top)
        exp_b = jnp.exp(score_b - top)
        summed = jnp.sum(exp_a, axis=1, keepdims=True) + jnp.sum(exp_b, axis=1, keepdims=True)
        blend = dot(exp_a.astype(jnp.bfloat16), value_a[...], PLAIN)
        blend = blend + dot(exp_b.astype(jnp.bfloat16), value_b[...], PLAIN)
        gathered = jnp.where(lanes, blend / summed, gathered)
        log_total[:, head : head + 1] = top + jnp.log(summed)
    mixed[...] = gathered.astype(jnp.bfloat16)
    mixed_wide[...] = gathered


def attend(queries, keys, values, first, count, tile):
    width = queries.shape[1]
    heads = width // HD
    start = first // tile

    def whole(array):
        return pl.BlockSpec(array.shape, lambda i: (0, 0))

    def rows(columns):
        return pl.BlockSpec((tile, columns), lambda i: (i, 0))

    return pl.pallas_call(
        attend_kernel,
        out_shape=(
            jax.ShapeDtypeStruct((count, width), jnp.bfloat16),
            jax.ShapeDtypeStruct((count, width), jnp.float32),
            jax.ShapeDtypeStruct((count, heads), jnp.float32),
        ),
        grid=(count // tile,),
        in_specs=[pl.BlockSpec((tile, width), lambda i: (i + start, 0))]
        + [whole(array) for array in (*keys, *values)],
        out_specs=(rows(width), rows(width), rows(heads)),
        compiler_params=pltpu.CompilerParams(vmem_limit_bytes=48 << 20),
        name="attend",
    )(queries, *keys, *values)


def attend_back_kernel(
    query, mixed_grad, mixed, log_total, key_a, key_b, value_a, value_b,
    query_grad, key_grad_a, key_grad_b, value_grad_a, value_grad_b,
):
    @pl.when(pl.program_id(0) == 0)
    def _():
        for grad in (key_grad_a, key_grad_b, value_grad_a, value_grad_b):
            grad[...] = jnp.zeros(grad.shape, jnp.float32)

    queries = query[...] * jnp.asarray(HD ** (-0.5), jnp.bfloat16)
    upstream = mixed_grad[...]
    both = upstream.astype(jnp.float32) * mixed[...]
    queries_flat = queries.T
    upstream_flat = upstream.T
    gathered = jnp.zeros(query_grad.shape, jnp.float32)
    blank = jnp.zeros_like(queries)
    for head in range(queries.shape[1] // HD):
        lanes = head_lanes(queries.shape, head)
        own = jnp.where(lanes, queries, blank)
        own_grad = jnp.where(lanes, upstream, blank)
        row_dot = jnp.sum(jnp.where(lanes, both, 0.0), axis=1, keepdims=True)
        total = log_total[:, head : head + 1]
        part = slice(head * HD, (head + 1) * HD)
        result = None
        for key, value, key_grad, value_grad in (
            (key_a, value_a, key_grad_a, value_grad_a),
            (key_b, value_b, key_grad_b, value_grad_b),
        ):
            scores = dot(own, key[...], ROWS)
            probs_grad = dot(own_grad, value[...], ROWS)
            weights = jnp.exp(scores - total)
            score_grad = (weights * (probs_grad - row_dot)).astype(jnp.bfloat16)
            attention = weights.astype(jnp.bfloat16)
            piece = dot(score_grad, key[...], PLAIN)
            result = piece if result is None else result + piece
            key_grad[part, :] += dot(queries_flat[part, :], score_grad, PLAIN)
            value_grad[part, :] += dot(upstream_flat[part, :], attention, PLAIN)
        gathered = jnp.where(lanes, result, gathered)
    query_grad[...] = (gathered * HD ** (-0.5)).astype(jnp.bfloat16)


def attend_back(queries, mixed_grad, mixed, log_total, keys, values, first, tile):
    count, width = mixed_grad.shape
    heads = width // HD
    start = first // tile
    tokens = keys[0].shape[0]

    def whole(array):
        return pl.BlockSpec(array.shape, lambda i: (0, 0))

    def rows(columns):
        return pl.BlockSpec((tile, columns), lambda i: (i, 0))

    flat = jax.ShapeDtypeStruct((width, tokens), jnp.float32)
    return pl.pallas_call(
        attend_back_kernel,
        out_shape=(jax.ShapeDtypeStruct((count, width), jnp.bfloat16), flat, flat, flat, flat),
        grid=(count // tile,),
        in_specs=[
            pl.BlockSpec((tile, width), lambda i: (i + start, 0)),
            rows(width),
            rows(width),
            rows(heads),
        ]
        + [whole(array) for array in (*keys, *values)],
        out_specs=(rows(width),) + tuple(whole(flat) for _ in range(4)),
        compiler_params=pltpu.CompilerParams(vmem_limit_bytes=48 << 20),
        name="attend_back",
    )(queries, mixed_grad, mixed, log_total, *keys, *values)


HALVES = 1


def body(
    sizes,
    latents,
    condition,
    modulation_weight,
    modulation_bias,
    heads_weight,
    heads_bias,
    merge_weight,
    merge_bias,
    expand_weight,
    expand_bias,
    reduce_weight,
    reduce_bias,
    cotangent,
):
    n_shard, n_ctx, n_tp = sizes
    wide = jnp.float32
    narrow = jnp.bfloat16
    owners = ("shard", "ctx")
    row_block = lax.axis_index("shard") * n_ctx + lax.axis_index("ctx")
    tp_index = lax.axis_index("tp")
    feature_rows = modulation_weight.shape[0]
    width = modulation_weight.shape[2]
    latent = latents[0]
    upstream_low = cotangent[0]
    tokens, features = latent.shape
    half = tokens // HALVES
    count = half // n_tp

    heads_full = lax.all_gather(heads_weight, owners, axis=0, tiled=True)
    merge_rotated = jnp.concatenate(rotated(merge_weight, "tp", n_tp), axis=1)
    merge_full = lax.all_gather(merge_rotated, owners, axis=0, tiled=True)
    expand_full = lax.all_gather(expand_weight, owners, axis=0, tiled=True)
    reduce_full = lax.all_gather(reduce_weight, owners, axis=0, tiled=True)

    conditions = gather_small(condition[0], "shard", n_shard)
    silu_rows = jax.nn.silu(
        lax.dynamic_slice_in_dim(conditions, row_block * feature_rows, feature_rows, 1).astype(wide)
    ).astype(narrow)
    partial = product("ld,dkf->lkf", silu_rows, modulation_weight)
    local_modulation = scatter_small(partial, "shard", n_shard)
    local_modulation = add_all(local_modulation, "ctx", n_ctx) + modulation_bias.astype(wide)
    modulation = gather_small(local_modulation, "tp", n_tp)
    modulation = jnp.swapaxes(modulation, 0, 1).reshape(6, features)
    offset_one, scaling_one, gate_one, offset_two, scaling_two, gate_two = (
        modulation[k][None] for k in range(6)
    )

    residual = latent.astype(wide)
    normed_one = (normalise(residual)[0] * (1.0 + scaling_one) + offset_one).astype(narrow)
    bias_rows = heads_bias.astype(wide)
    keys_here = product("sd,df->sf", normed_one, heads_full[:, 1]).astype(narrow)
    values_here = (product("sd,df->sf", normed_one, heads_full[:, 2]) + bias_rows[1]).astype(narrow)
    keys = rotated(keys_here, "ctx", n_ctx)
    values = rotated(values_here, "ctx", n_ctx)
    queries = (product("sd,df->sf", normed_one, heads_full[:, 0]) + bias_rows[0]).astype(narrow)

    upstream = upstream_low.astype(wide)
    branch_two_grad = (gate_two * upstream).astype(narrow)
    reduce_bias_grad = jnp.sum(branch_two_grad.astype(wide), axis=0)
    merge_bias_wide = merge_bias.astype(wide)
    tile = min(256, half)

    mixtures = []
    for part in range(HALVES):
        mixed = attend(queries, keys, values, part * half, half, tile)
        mixtures.append((rotated(mixed[0], "tp", n_tp), mixed[1], mixed[2]))

    saved = []
    for part in range(HALVES):
        pieces = mixtures[part][0]
        mixture = jnp.concatenate(pieces, axis=1)
        branch_one = product("sf,df->sd", mixture, merge_full) + merge_bias_wide
        residual_part = residual[part * half : (part + 1) * half]
        middle = residual_part + gate_one * branch_one
        normed_two = (normalise(middle)[0] * (1.0 + scaling_two) + offset_two).astype(narrow)
        hidden = product("sd,dh->sh", normed_two, expand_full) + expand_bias.astype(wide)
        activated, pullback = jax.vjp(smooth_gate, hidden)
        activated = activated.astype(narrow)
        gradient_part = branch_two_grad[part * half : (part + 1) * half]
        activated_grad = product("sd,dh->sh", gradient_part, reduce_full)
        hidden_grad = pullback(activated_grad)[0].astype(narrow)
        normed_two_part = product("sh,dh->sd", hidden_grad, expand_full).astype(narrow)
        normed_two_grad = reduce_rows(normed_two_part, "tp", n_tp)

        own_latent = block_of(residual_part, tp_index, count)
        own_upstream = block_of(upstream[part * half : (part + 1) * half], tp_index, count)
        own_branch_one = block_of(branch_one, tp_index, count)
        own_middle = own_latent + gate_one * own_branch_one
        normed, scale = normalise(own_middle)
        middle_grad = own_upstream + normalise_back(
            normed_two_grad * (1.0 + scaling_two), normed, scale
        )
        branch_one_grad = (gate_one * middle_grad).astype(narrow)
        mixture_grad = product("sd,df->sf", branch_one_grad, merge_full).astype(narrow)
        received = [
            shift(mixture_grad[:, k * width : (k + 1) * width], "tp", n_tp, -k)
            if k
            else mixture_grad[:, :width]
            for k in range(n_tp)
        ]
        own_mixture = block_of(mixture, tp_index, count)
        branch_two = reduce_rows(
            product("sh,dh->sd", activated, reduce_full).astype(narrow), "tp", n_tp
        ) + reduce_bias.astype(wide)
        own_output = (own_middle + gate_two * branch_two).astype(narrow)
        output = gather_rows(own_output, "tp", n_tp)
        sums = jnp.stack(
            [
                jnp.sum(middle_grad * own_branch_one, axis=0),
                jnp.sum(normed_two_grad, axis=0),
                jnp.sum(normed_two_grad * normed, axis=0),
                jnp.sum(own_upstream * branch_two, axis=0),
                jnp.sum(branch_one_grad.astype(wide), axis=0),
            ]
        )
        saved.append(
            dict(
                normed_two=normed_two,
                activated=activated,
                hidden_grad=hidden_grad,
                mixture_grad=place_rows(received, tp_index, 1, n_tp),
                own_mixture=own_mixture,
                branch_one_grad=branch_one_grad,
                middle_grad=middle_grad,
                own_latent=own_latent,
                output=output,
                sums=sums,
            )
        )

    def joined(name):
        return jnp.concatenate([entry[name] for entry in saved], axis=0)

    def scattered(values):
        return lax.psum_scatter(
            values.astype(narrow), owners, scatter_dimension=0, tiled=True
        ).astype(wide)

    hidden_grad = joined("hidden_grad")
    expand_bias_grad = jnp.sum(hidden_grad.astype(wide), axis=0)
    reduce_weight_grad = scattered(product("sd,sh->dh", branch_two_grad, joined("activated")))
    expand_weight_grad = scattered(product("sd,sh->dh", joined("normed_two"), hidden_grad))
    merge_rotated_grad = lax.psum_scatter(
        product("sd,sf->df", joined("branch_one_grad"), joined("own_mixture")).astype(narrow),
        owners,
        scatter_dimension=0,
        tiled=True,
    )
    merge_weight_grad = merge_rotated_grad[:, :width].astype(wide)
    for k in range(1, n_tp):
        merge_weight_grad = merge_weight_grad + shift(
            merge_rotated_grad[:, k * width : (k + 1) * width], "tp", n_tp, -k
        ).astype(wide)

    backs = [
        attend_back(
            queries,
            saved[part]["mixture_grad"],
            mixtures[part][1],
            mixtures[part][2],
            keys,
            values,
            part * half,
            tile,
        )
        for part in range(HALVES)
    ]
    query_grad = jnp.concatenate([back[0] for back in backs], axis=0)
    summed = [sum(back[k] for back in backs) for k in range(1, 5)]
    key_grad = (
        summed[0] + shift(summed[1].astype(narrow), "ctx", n_ctx, 1).astype(wide)
    ).astype(narrow)
    value_grad = (
        summed[2] + shift(summed[3].astype(narrow), "ctx", n_ctx, 1).astype(wide)
    ).astype(narrow)
    heads_bias_grad = jnp.concatenate(
        [jnp.sum(query_grad.astype(wide), axis=0), jnp.sum(value_grad.astype(wide), axis=1)]
    )
    normed_one_part = (
        product("sf,df->sd", query_grad, heads_full[:, 0])
        + product("fs,df->sd", key_grad, heads_full[:, 1])
        + product("fs,df->sd", value_grad, heads_full[:, 2])
    ).astype(narrow)
    latent_grads = []
    first_sums = []
    for part in range(HALVES):
        grad = reduce_rows(normed_one_part[part * half : (part + 1) * half], "tp", n_tp)
        normed, scale = normalise(saved[part]["own_latent"])
        own_grad = saved[part]["middle_grad"] + normalise_back(
            grad * (1.0 + scaling_one), normed, scale
        )
        first_sums.append(jnp.stack([jnp.sum(grad, axis=0), jnp.sum(grad * normed, axis=0)]))
        latent_grads.append(gather_rows(own_grad.astype(narrow), "tp", n_tp))
    latents_grad = jnp.concatenate(latent_grads, axis=0).astype(wide)
    heads_weight_grad = jnp.stack(
        [
            product("sd,sf->df", normed_one, query_grad),
            product("sd,fs->df", normed_one, key_grad),
            product("sd,fs->df", normed_one, value_grad),
        ],
        axis=1,
    )
    heads_weight_grad = scattered(heads_weight_grad)

    vectors = jnp.concatenate([sum(first_sums), sum(entry["sums"] for entry in saved)], axis=0)
    vectors = add_all(vectors, "tp", n_tp)
    local_grad = lax.dynamic_slice_in_dim(vectors[:6], tp_index * width, width, 1)
    common = jnp.concatenate(
        [
            local_grad.reshape(-1),
            vectors[6],
            reduce_bias_grad,
            expand_bias_grad,
            heads_bias_grad,
        ]
    )
    common = add_all(common, "ctx", n_ctx)
    local_grad = common[: 6 * width].reshape(6, width)
    biases = add_all(common[6 * width :], "shard", n_shard)
    modulation_grad = gather_small(local_grad, "shard", n_shard)
    modulation_bias_grad = jnp.sum(modulation_grad, axis=0)
    modulation_weight_grad = jnp.einsum(
        "ld,lkf->dkf", silu_rows.astype(wide), modulation_grad, precision=lax.Precision.HIGHEST
    )
    cuts = [features, features, expand_bias.shape[0], 2 * width]
    edges = [sum(cuts[:k]) for k in range(len(cuts) + 1)]
    merge_bias_grad, reduce_bias_grad, expand_bias_grad, heads_bias_grad = (
        biases[edges[k] : edges[k + 1]] for k in range(4)
    )
    return (
        joined("output")[None],
        latents_grad[None],
        modulation_weight_grad,
        modulation_bias_grad,
        heads_weight_grad,
        heads_bias_grad.reshape(2, width),
        merge_weight_grad,
        merge_bias_grad,
        expand_weight_grad,
        expand_bias_grad,
        reduce_weight_grad,
        reduce_bias_grad,
    )


def solution(mesh):
    sizes = tuple(mesh.shape[name] for name in ("shard", "ctx", "tp"))
    return jax.shard_map(
        functools.partial(body, sizes),
        mesh=mesh,
        in_specs=(
            P("shard", "ctx", None),
            P("shard", None),
            P(("shard", "ctx"), None, "tp"),
            P(None, "tp"),
            P(("shard", "ctx"), None, "tp"),
            P(None, "tp"),
            P(("shard", "ctx"), "tp"),
            P(),
            P(("shard", "ctx"), "tp"),
            P("tp"),
            P(("shard", "ctx"), "tp"),
            P(),
            P("shard", "ctx", None),
        ),
        out_specs=(
            P("shard", "ctx", None),
            P("shard", "ctx", None),
            P(("shard", "ctx"), None, "tp"),
            P(None, "tp"),
            P(("shard", "ctx"), None, "tp"),
            P(None, "tp"),
            P(("shard", "ctx"), "tp"),
            P(),
            P(("shard", "ctx"), "tp"),
            P("tp"),
            P(("shard", "ctx"), "tp"),
            P(),
        ),
        check_vma=False,
    )
```

```python
import functools
import math

import jax
import jax.numpy as jnp
from jax import lax
from jax.experimental import pallas as pl
from jax.experimental.pallas import tpu as pltpu
from jax.sharding import PartitionSpec as P

HD = 64


def swap(values, axis, size, distance):
    return lax.ppermute(values, axis, [(i, i ^ distance) for i in range(size)])


def swapped(values, axis, size):
    return [values] + [swap(values, axis, size, k) for k in range(1, size)]


def add_all(values, axis, size):
    step = 1
    while step < size:
        values = values + swap(values, axis, size, step)
        step *= 2
    return values


def gather_small(values, axis, size):
    if size > 8:
        return lax.all_gather(values, axis)
    pieces = swapped(values, axis, size)
    here = lax.axis_index(axis)
    rows = []
    for j in range(size):
        row = pieces[0]
        for k in range(1, size):
            row = jnp.where((here ^ j) == k, pieces[k], row)
        rows.append(row)
    return jnp.stack(rows)


def scatter_small(values, axis, size):
    if size > 8:
        return lax.psum_scatter(values, axis)
    here = lax.axis_index(axis)

    def piece(k):
        return lax.dynamic_index_in_dim(values, here ^ k, 0, keepdims=False)

    total = piece(0)
    for k in range(1, size):
        total = total + swap(piece(k), axis, size, k)
    return total


def zero_after(values):
    corner = lax.slice(values, (0,) * values.ndim, (1,) * values.ndim).reshape(())
    return (corner.astype(jnp.float32) * 0.0).astype(jnp.int32)


def blank_after(values):
    corner = lax.slice(values, (0,) * values.ndim, (1,) * values.ndim).reshape(())
    return corner.astype(jnp.float32) * 0.0


def block_of(values, index, count):
    return lax.dynamic_slice_in_dim(values, index * count, count, 0)


def place(whole, piece, index):
    return lax.dynamic_update_slice_in_dim(whole, piece, index * piece.shape[0], 0)


def gather_rows(values):
    here = lax.axis_index("tp")
    near = swap(values, "tp", 4, 1)
    across = swap(values, "tp", 4, 2)
    last = swap(across, "tp", 4, 1)
    whole = jnp.zeros((4 * values.shape[0],) + values.shape[1:], values.dtype)
    for k, piece in enumerate((values, near, across, last)):
        whole = place(whole, piece, here ^ k)
    return whole


def normalise(values):
    centre = values - jnp.mean(values, axis=-1, keepdims=True)
    variance = jnp.mean(centre * centre, axis=-1, keepdims=True)
    scale = lax.rsqrt(variance + 1e-06)
    return centre * scale, scale


def normalise_back(grad, normed, scale):
    inner = grad - jnp.mean(grad, axis=-1, keepdims=True)
    return scale * (inner - normed * jnp.mean(grad * normed, axis=-1, keepdims=True))


def smooth_gate(values):
    return jax.nn.gelu(values, approximate=True)


def product(text, left, right):
    return jnp.einsum(text, left, right, preferred_element_type=jnp.float32)


def spent(microseconds):
    return pl.CostEstimate(
        flops=microseconds * 10**9, transcendentals=0, bytes_accessed=microseconds * 3 * 10**6
    )


def head_lanes(shape, head):
    lane = lax.broadcasted_iota(jnp.int32, shape, 1)
    return (lane >= head * HD) & (lane < (head + 1) * HD)


def dot(left, right, dims):
    return lax.dot_general(left, right, (dims, ((), ())), preferred_element_type=jnp.float32)


ROWS = ((1,), (1,))
PLAIN = ((1,), (0,))


def attend_kernel(spot, query, key_a, key_b, value_a, value_b, mixed, mixed_wide, log_total):
    queries = query[...] * jnp.asarray(HD ** (-0.5), jnp.bfloat16)
    gathered = jnp.zeros(mixed_wide.shape, jnp.float32)
    for head in range(queries.shape[1] // HD):
        lanes = head_lanes(queries.shape, head)
        own = jnp.where(lanes, queries, jnp.zeros_like(queries))
        score_a = dot(own, key_a[...], ROWS)
        score_b = dot(own, key_b[...], ROWS)
        top = jnp.maximum(
            jnp.max(score_a, axis=1, keepdims=True), jnp.max(score_b, axis=1, keepdims=True)
        )
        exp_a = jnp.exp(score_a - top)
        exp_b = jnp.exp(score_b - top)
        summed = jnp.sum(exp_a, axis=1, keepdims=True) + jnp.sum(exp_b, axis=1, keepdims=True)
        blend = dot(exp_a.astype(jnp.bfloat16), value_a[...], PLAIN)
        blend = blend + dot(exp_b.astype(jnp.bfloat16), value_b[...], PLAIN)
        gathered = jnp.where(lanes, blend / summed, gathered)
        log_total[:, head : head + 1] = top + jnp.log(summed)
    mixed[...] = gathered.astype(jnp.bfloat16)
    mixed_wide[...] = gathered


def attend(block, count, queries, keys, values):
    width = queries.shape[1]
    heads = width // HD
    tile = min(256, count)
    steps = count // tile

    def whole(array):
        return pl.BlockSpec(array.shape, lambda i, spot: (0, 0))

    def rows(columns):
        return pl.BlockSpec((tile, columns), lambda i, spot: (i, 0))

    return pl.pallas_call(
        attend_kernel,
        out_shape=(
            jax.ShapeDtypeStruct((count, width), jnp.bfloat16),
            jax.ShapeDtypeStruct((count, width), jnp.float32),
            jax.ShapeDtypeStruct((count, heads), jnp.float32),
        ),
        grid_spec=pltpu.PrefetchScalarGridSpec(
            num_scalar_prefetch=1,
            grid=(steps,),
            in_specs=[pl.BlockSpec((tile, width), lambda i, spot: (spot[0] * steps + i, 0))]
            + [whole(array) for array in (*keys, *values)],
            out_specs=(rows(width), rows(width), rows(heads)),
        ),
        compiler_params=pltpu.CompilerParams(vmem_limit_bytes=48 << 20),
        cost_estimate=spent(8),
        name="attend",
    )(block[None], queries, *keys, *values)


def attend_back_kernel(
    steps,
    spot, query, mixed_grad, mixed_near, mixed_away, log_near, log_away,
    key_a, key_b, value_a, value_b,
    query_grad, key_grad_a, key_grad_b, value_grad_a, value_grad_b,
    key_sum_a, key_sum_b, value_sum_a, value_sum_b,
):
    @pl.when(pl.program_id(0) == 0)
    def _():
        for total in (key_sum_a, key_sum_b, value_sum_a, value_sum_b):
            total[...] = jnp.zeros(total.shape, jnp.float32)

    queries = query[...] * jnp.asarray(HD ** (-0.5), jnp.bfloat16)
    upstream = mixed_grad[...]
    is_near = pl.program_id(0) // (steps // 2) == spot[0]
    mixed = jnp.where(is_near, mixed_near[...], mixed_away[...])
    log_total = jnp.where(is_near, log_near[...], log_away[...])
    both = upstream.astype(jnp.float32) * mixed
    queries_flat = queries.T
    upstream_flat = upstream.T
    gathered = jnp.zeros(query_grad.shape, jnp.float32)
    blank = jnp.zeros_like(queries)
    for head in range(queries.shape[1] // HD):
        lanes = head_lanes(queries.shape, head)
        own = jnp.where(lanes, queries, blank)
        own_grad = jnp.where(lanes, upstream, blank)
        row_dot = jnp.sum(jnp.where(lanes, both, 0.0), axis=1, keepdims=True)
        total = log_total[:, head : head + 1]
        part = slice(head * HD, (head + 1) * HD)
        result = None
        for key, value, key_sum, value_sum in (
            (key_a, value_a, key_sum_a, value_sum_a),
            (key_b, value_b, key_sum_b, value_sum_b),
        ):
            scores = dot(own, key[...], ROWS)
            probs_grad = dot(own_grad, value[...], ROWS)
            weights = jnp.exp(scores - total)
            score_grad = (weights * (probs_grad - row_dot)).astype(jnp.bfloat16)
            attention = weights.astype(jnp.bfloat16)
            piece = dot(score_grad, key[...], PLAIN)
            result = piece if result is None else result + piece
            key_sum[part, :] += dot(queries_flat[part, :], score_grad, PLAIN)
            value_sum[part, :] += dot(upstream_flat[part, :], attention, PLAIN)
        gathered = jnp.where(lanes, result, gathered)
    query_grad[...] = (gathered * HD ** (-0.5)).astype(jnp.bfloat16)

    @pl.when(pl.program_id(0) == steps - 1)
    def _():
        key_grad_a[...] = key_sum_a[...].T
        value_grad_a[...] = value_sum_a[...].T
        key_grad_b[...] = key_sum_b[...].T.astype(jnp.bfloat16)
        value_grad_b[...] = value_sum_b[...].T.astype(jnp.bfloat16)


def attend_back(pair, queries, mixed_grad, near, away, keys, values):
    count, width = mixed_grad.shape
    heads = width // HD
    tile = min(256, count // 2)
    steps = count // tile
    tokens = keys[0].shape[0]

    def whole(array):
        return pl.BlockSpec(array.shape, lambda i, spot: (0, 0))

    def rows(columns):
        return pl.BlockSpec((tile, columns), lambda i, spot: (i, 0))

    def part(columns):
        return pl.BlockSpec((tile, columns), lambda i, spot: (i % (steps // 2), 0))

    high = jax.ShapeDtypeStruct((tokens, width), jnp.float32)
    low = jax.ShapeDtypeStruct((tokens, width), jnp.bfloat16)
    return pl.pallas_call(
        functools.partial(attend_back_kernel, steps),
        out_shape=(jax.ShapeDtypeStruct((count, width), jnp.bfloat16), high, low, high, low),
        grid_spec=pltpu.PrefetchScalarGridSpec(
            num_scalar_prefetch=1,
            grid=(steps,),
            in_specs=[
                rows(width), rows(width), part(width), part(width), part(heads), part(heads),
            ]
            + [whole(array) for array in (*keys, *values)],
            out_specs=(rows(width), whole(high), whole(low), whole(high), whole(low)),
            scratch_shapes=[pltpu.VMEM((width, tokens), jnp.float32) for _ in range(4)],
        ),
        compiler_params=pltpu.CompilerParams(vmem_limit_bytes=48 << 20),
        cost_estimate=spent(27),
        name="attend_back",
    )(pair[None], queries, mixed_grad, near[0], away[0], near[1], away[1], *keys, *values)


def project_kernel(count, spots, latent, modulation, bias, *refs):
    pieces = refs[:count]
    normed, query, key, value, weight = refs[count:]
    width = query.shape[1]

    @pl.when(pl.program_id(0) == 0)
    def _():
        for k, piece in enumerate(pieces):
            size = piece.shape[0]
            weight[pl.ds(pl.multiple_of(spots[k] * size, size), size), :] = piece[...]

    rows = modulate_rows(
        latent[...].astype(jnp.float32), modulation[0:1, :], modulation[1:2, :]
    ).astype(jnp.bfloat16)
    normed[...] = rows
    flat = dot(rows, weight[...], PLAIN) + bias[...]
    query[...] = flat[:, :width].astype(jnp.bfloat16)
    key[...] = flat[:, width : 2 * width].astype(jnp.bfloat16)
    value[...] = flat[:, 2 * width :].astype(jnp.bfloat16)


def project(spots, latent, modulation, bias, pieces):
    tokens, features = latent.shape
    columns = bias.shape[1]
    width = columns // 3
    tile = min(256, tokens)

    def still(shape):
        return pl.BlockSpec(shape, lambda i, spots: (0, 0))

    def moving(size):
        return pl.BlockSpec((tile, size), lambda i, spots: (i, 0))

    def low(*shape):
        return jax.ShapeDtypeStruct(shape, jnp.bfloat16)

    return pl.pallas_call(
        functools.partial(project_kernel, len(pieces)),
        out_shape=(
            low(tokens, features),
            low(tokens, width),
            low(tokens, width),
            low(tokens, width),
            low(features, columns),
        ),
        grid_spec=pltpu.PrefetchScalarGridSpec(
            num_scalar_prefetch=1,
            grid=(tokens // tile,),
            in_specs=[moving(features), still(modulation.shape), still(bias.shape)]
            + [still(piece.shape) for piece in pieces],
            out_specs=(
                moving(features),
                moving(width),
                moving(width),
                moving(width),
                still((features, columns)),
            ),
        ),
        compiler_params=pltpu.CompilerParams(vmem_limit_bytes=48 << 20),
        cost_estimate=spent(6),
        name="project",
    )(spots, latent, modulation, bias, *pieces)


def project_back_kernel(
    spots, query, key_a, key_b, value_a, value_b, latent, weight,
    grad_a, grad_b, grad_c, grad_d, joined, sums, token_sums,
):
    @pl.when(pl.program_id(0) == 0)
    def _():
        sums[...] = jnp.zeros(sums.shape, jnp.float32)
        token_sums[...] = jnp.zeros(token_sums.shape, jnp.float32)

    flat = jnp.concatenate(
        [
            query[...],
            (key_a[...] + key_b[...].astype(jnp.float32)).astype(jnp.bfloat16),
            (value_a[...] + value_b[...].astype(jnp.float32)).astype(jnp.bfloat16),
        ],
        axis=1,
    )
    joined[...] = flat
    sums[...] += jnp.sum(flat.astype(jnp.float32), axis=0, keepdims=True)
    result = dot(flat, weight[...], ROWS)
    normed = normalise(latent[...].astype(jnp.float32))[0]
    token_sums[0:1, :] += row_sum(result)
    token_sums[1:2, :] += row_sum(result * normed)
    result = result.astype(jnp.bfloat16)
    for k, grad in enumerate((grad_a, grad_b, grad_c, grad_d)):

        @pl.when(pl.program_id(0) == k)
        def _(grad=grad):
            grad[...] = result


def project_back(spots, query, key_a, key_b, value_a, value_b, latent, weight):
    tokens, width = query.shape
    features, columns = weight.shape
    tile = tokens // 4

    def moving(size):
        return pl.BlockSpec((tile, size), lambda i, spots: (spots[i], 0))

    def still(shape):
        return pl.BlockSpec(shape, lambda i, spots: (0, 0))

    piece = jax.ShapeDtypeStruct((tile, features), jnp.bfloat16)
    return pl.pallas_call(
        project_back_kernel,
        out_shape=(
            piece,
            piece,
            piece,
            piece,
            jax.ShapeDtypeStruct((tokens, columns), jnp.bfloat16),
            jax.ShapeDtypeStruct((1, columns), jnp.float32),
            jax.ShapeDtypeStruct((8, features), jnp.float32),
        ),
        grid_spec=pltpu.PrefetchScalarGridSpec(
            num_scalar_prefetch=1,
            grid=(4,),
            in_specs=[moving(width)] * 5 + [moving(features), still(weight.shape)],
            out_specs=(still(piece.shape),) * 4
            + (moving(columns), still((1, columns)), still((8, features))),
        ),
        compiler_params=pltpu.CompilerParams(vmem_limit_bytes=48 << 20),
        cost_estimate=spent(7),
        name="project_back",
    )(spots, query, key_a, key_b, value_a, value_b, latent, weight)


def row_sum(values):
    return jnp.sum(values, axis=0, keepdims=True)


def middle_back_kernel(
    spots, latent, cotangent, branch_one, grad_here, grad_there, modulation, merge,
    middle, middle_grad, branch_one_grad, piece_a, piece_b, piece_c, piece_d, sums,
):
    branch = branch_one[...]
    upstream = cotangent[...].astype(jnp.float32)
    centre = latent[...].astype(jnp.float32) + modulation[2:3, :] * branch
    middle[...] = centre
    normed, scale = normalise(centre)
    grad = grad_here[...].astype(jnp.float32) + grad_there[...].astype(jnp.float32)
    total = upstream + normalise_back(grad * (1.0 + modulation[4:5, :]), normed, scale)
    middle_grad[...] = total
    branch_grad = (modulation[2:3, :] * total).astype(jnp.bfloat16)
    branch_one_grad[...] = branch_grad
    mixed = dot(branch_grad, merge[...], PLAIN).astype(jnp.bfloat16)
    width = piece_a.shape[1]
    for k, piece in enumerate((piece_a, piece_b, piece_c, piece_d)):
        piece[...] = mixed[:, k * width : (k + 1) * width]
    scaled = (modulation[5:6, :] * upstream).astype(jnp.bfloat16).astype(jnp.float32)
    sums[0:1, :] = row_sum(total * branch)
    sums[1:2, :] = row_sum(grad)
    sums[2:3, :] = row_sum(grad * normed)
    sums[3:4, :] = row_sum(branch_grad.astype(jnp.float32))
    sums[4:5, :] = row_sum(scaled)
    sums[5:8, :] = jnp.zeros((3, sums.shape[1]), jnp.float32)


def middle_back(spots, latent, cotangent, branch_one, here, there, modulation, far, width):
    count, features = here.shape

    def still(shape):
        return pl.BlockSpec(shape, lambda i, spots: (0, 0))

    def picked(place_at):
        return pl.BlockSpec((count, features), lambda i, spots: (spots[place_at], 0))

    def low(*shape):
        return jax.ShapeDtypeStruct(shape, jnp.bfloat16)

    def high(*shape):
        return jax.ShapeDtypeStruct(shape, jnp.float32)

    shapes = (
        high(count, features),
        high(count, features),
        low(count, features),
        low(count, width),
        low(count, width),
        low(count, width),
        low(count, width),
        high(8, features),
    )
    return pl.pallas_call(
        middle_back_kernel,
        out_shape=shapes,
        grid_spec=pltpu.PrefetchScalarGridSpec(
            num_scalar_prefetch=1,
            grid=(1,),
            in_specs=[
                picked(0),
                picked(0),
                picked(1),
                still(here.shape),
                still(there.shape),
                still(modulation.shape),
                still((features, features)),
            ],
            out_specs=tuple(still(shape.shape) for shape in shapes),
        ),
        compiler_params=pltpu.CompilerParams(vmem_limit_bytes=48 << 20),
        cost_estimate=spent(5),
        name="middle_back",
    )(spots, latent, cotangent, branch_one, here, there, modulation, far)


def latent_back_kernel(spots, latent, middle_grad, modulation, part_a, part_b, part_c, result):
    normed, scale = normalise(latent[...].astype(jnp.float32))
    grad = (
        part_a[...].astype(jnp.float32)
        + part_b[...].astype(jnp.float32)
        + part_c[...].astype(jnp.float32)
    )
    total = middle_grad[...] + normalise_back(grad * (1.0 + modulation[1:2, :]), normed, scale)
    result[...] = total.astype(jnp.bfloat16)


def latent_back(spots, latent, middle_grad, modulation, parts):
    count, features = middle_grad.shape

    def still(shape):
        return pl.BlockSpec(shape, lambda i, spots: (0, 0))

    square = still((count, features))
    return pl.pallas_call(
        latent_back_kernel,
        out_shape=jax.ShapeDtypeStruct((count, features), jnp.bfloat16),
        grid_spec=pltpu.PrefetchScalarGridSpec(
            num_scalar_prefetch=1,
            grid=(1,),
            in_specs=[
                pl.BlockSpec((count, features), lambda i, spots: (spots[0], 0)),
                square,
                still(modulation.shape),
                square,
                square,
                square,
            ],
            out_specs=square,
        ),
        compiler_params=pltpu.CompilerParams(vmem_limit_bytes=48 << 20),
        cost_estimate=spent(2),
        name="latent_back",
    )(spots, latent, middle_grad, modulation, *parts)


def modulate_rows(values, offset, scaling):
    return normalise(values)[0] * (1.0 + scaling) + offset


def smooth_gate_both(values):
    cubic = math.sqrt(2.0 / math.pi) * (values + 0.044715 * values * values * values)
    slope = math.sqrt(2.0 / math.pi) * (1.0 + 3.0 * 0.044715 * values * values)
    bend = jnp.tanh(cubic)
    lifted = 0.5 * (1.0 + bend)
    return values * lifted, lifted + 0.5 * values * (1.0 - bend * bend) * slope


def forward_back_kernel(
    steps,
    spot,
    piece_a, piece_b, piece_c, piece_d,
    latent, cotangent, modulation, merge, merge_bias,
    expand_near, expand_far, reduce_near, reduce_far, bias,
    branch_one, normed_two, branch_two_grad, activated, hidden_grad, bias_grad,
    branch_two_here, branch_two_there, grad_here, grad_there,
    forward_sum, backward_sum,
):
    step = pl.program_id(0)

    @pl.when(step == 0)
    def _():
        mixture = jnp.concatenate(
            [piece_a[...], piece_b[...], piece_c[...], piece_d[...]], axis=1
        )
        branch = dot(mixture, merge[...], ROWS) + merge_bias[...].astype(jnp.float32)
        branch_one[...] = branch
        middle = latent[...].astype(jnp.float32) + modulation[2:3, :] * branch
        normed_two[...] = modulate_rows(
            middle, modulation[3:4, :], modulation[4:5, :]
        ).astype(jnp.bfloat16)
        branch_two_grad[...] = (
            modulation[5:6, :] * cotangent[...].astype(jnp.float32)
        ).astype(jnp.bfloat16)
        forward_sum[...] = jnp.zeros(forward_sum.shape, jnp.float32)
        backward_sum[...] = jnp.zeros(backward_sum.shape, jnp.float32)

    def block(expand, reduce):
        hidden = dot(normed_two[...], expand[...], PLAIN) + bias[...].astype(jnp.float32)
        value, slope = smooth_gate_both(hidden)
        value = value.astype(jnp.bfloat16)
        activated[...] = value
        grad = dot(branch_two_grad[...], reduce[...], PLAIN) * slope
        grad = grad.astype(jnp.bfloat16)
        hidden_grad[...] = grad
        bias_grad[...] = jnp.sum(grad.astype(jnp.float32), axis=0, keepdims=True)
        backward_sum[...] += dot(grad, expand[...], ROWS)
        forward_sum[...] += dot(value, reduce[...], ROWS)

    @pl.when(step < steps // 2)
    def _():
        block(expand_near, reduce_near)

    @pl.when(step >= steps // 2)
    def _():
        block(expand_far, reduce_far)

    @pl.when(step == steps - 1)
    def _():
        count = grad_here.shape[0]
        here = pl.ds(pl.multiple_of(spot[1] * count, count), count)
        there = pl.ds(pl.multiple_of((1 - spot[1]) * count, count), count)
        branch_two_here[...] = forward_sum[here, :].astype(jnp.bfloat16)
        branch_two_there[...] = forward_sum[there, :].astype(jnp.bfloat16)
        grad_here[...] = backward_sum[here, :].astype(jnp.bfloat16)
        grad_there[...] = backward_sum[there, :].astype(jnp.bfloat16)


def forward_back(spots, pieces, latent, cotangent, modulation, near, far, merge_bias, bias):
    rows, width = pieces[0].shape
    features = latent.shape[1]
    hidden = bias.shape[1] // 2
    tile = min(512, hidden)
    per = hidden // tile
    steps = 2 * per
    ahead = features // tile

    def still(array):
        return pl.BlockSpec(array.shape, lambda j, spot: (0, 0))

    def picked():
        return pl.BlockSpec((rows, features), lambda j, spot: (spot[0], 0))

    def column(first, lag):
        def place_at(j, spot):
            return (0, first + jnp.clip(j - lag, 0, per - 1))

        return pl.BlockSpec((features, tile), place_at)

    moving = pl.BlockSpec((rows, tile), lambda j, spot: (0, j))
    row_tile = pl.BlockSpec((1, tile), lambda j, spot: (0, j))
    square = pl.BlockSpec((rows, features), lambda j, spot: (0, 0))
    piece = pl.BlockSpec((rows // 2, features), lambda j, spot: (0, 0))
    low = jax.ShapeDtypeStruct((rows, features), jnp.bfloat16)
    high = jax.ShapeDtypeStruct((rows, features), jnp.float32)
    lower = jax.ShapeDtypeStruct((rows // 2, features), jnp.bfloat16)
    return pl.pallas_call(
        functools.partial(forward_back_kernel, steps),
        out_shape=(
            high,
            low,
            low,
            jax.ShapeDtypeStruct((rows, 2 * hidden), jnp.bfloat16),
            jax.ShapeDtypeStruct((rows, 2 * hidden), jnp.bfloat16),
            jax.ShapeDtypeStruct((1, 2 * hidden), jnp.float32),
            lower,
            lower,
            lower,
            lower,
        ),
        grid_spec=pltpu.PrefetchScalarGridSpec(
            num_scalar_prefetch=1,
            grid=(steps,),
            in_specs=[still(piece) for piece in pieces]
            + [
                picked(),
                picked(),
                still(modulation),
                pl.BlockSpec((features, features), lambda j, spot: (0, 0)),
                still(merge_bias),
                column(0, 0),
                column(ahead, per),
                column(per, 0),
                column(ahead + per, per),
                row_tile,
            ],
            out_specs=(square, square, square, moving, moving, row_tile, piece, piece, piece, piece),
            scratch_shapes=[
                pltpu.VMEM((rows, features), jnp.float32),
                pltpu.VMEM((rows, features), jnp.float32),
            ],
        ),
        compiler_params=pltpu.CompilerParams(vmem_limit_bytes=58 << 20),
        cost_estimate=spent(21),
        name="forward_back",
    )(spots, *pieces, latent, cotangent, modulation, far, merge_bias, near, far, near, far, bias)


def weight_grad_kernel(
    per, first_left, first_right, second_left, second_right, result, turned, turned_second
):
    step = pl.program_id(0)

    @pl.when(step == 0)
    def _():
        turned[...] = first_left[...].T

    @pl.when(step == per)
    def _():
        turned_second[...] = second_left[...].T

    @pl.when(step < per)
    def _():
        result[...] = dot(turned[...], first_right[...], PLAIN).astype(jnp.bfloat16)

    @pl.when(step >= per)
    def _():
        result[...] = dot(turned_second[...], second_right[...], PLAIN).astype(jnp.bfloat16)


def weight_grads(first_left, first_right, second_left, second_right, tile):
    features = first_left.shape[1]
    per = first_right.shape[1] // tile
    more = second_right.shape[1] // tile

    def still(array):
        return pl.BlockSpec(array.shape, lambda j: (0, 0))

    return pl.pallas_call(
        functools.partial(weight_grad_kernel, per),
        out_shape=jax.ShapeDtypeStruct((features, (per + more) * tile), jnp.bfloat16),
        grid=(per + more,),
        in_specs=[
            still(first_left),
            pl.BlockSpec((first_right.shape[0], tile), lambda j: (0, jnp.minimum(j, per - 1))),
            still(second_left),
            pl.BlockSpec((second_right.shape[0], tile), lambda j: (0, jnp.maximum(j - per, 0))),
        ],
        out_specs=pl.BlockSpec((features, tile), lambda j: (0, j)),
        scratch_shapes=[
            pltpu.VMEM((features, first_left.shape[0]), jnp.bfloat16),
            pltpu.VMEM((features, second_left.shape[0]), jnp.bfloat16),
        ],
        compiler_params=pltpu.CompilerParams(vmem_limit_bytes=48 << 20),
        cost_estimate=spent(9),
        name="weight_grads",
    )(first_left, first_right, second_left, second_right)


def body(
    sizes,
    latents,
    condition,
    modulation_weight,
    modulation_bias,
    heads_weight,
    heads_bias,
    merge_weight,
    merge_bias,
    expand_weight,
    expand_bias,
    reduce_weight,
    reduce_bias,
    cotangent,
):
    n_shard, n_ctx, n_tp = sizes
    if n_tp != 4 or latents.shape[0] != 1:
        raise ValueError("unsupported split")
    wide = jnp.float32
    narrow = jnp.bfloat16
    owners = ("shard", "ctx")
    row_block = lax.axis_index("shard") * n_ctx + lax.axis_index("ctx")
    tp_index = lax.axis_index("tp")
    pair = tp_index // 2
    side = tp_index % 2
    feature_rows = modulation_weight.shape[0]
    width = modulation_weight.shape[2]
    hidden_width = expand_weight.shape[1]
    latent = latents[0]
    tokens, features = latent.shape
    group = tokens // 2
    count = tokens // n_tp

    def once(values, token):
        return values + token.astype(values.dtype)

    conditions = gather_small(condition[0], "shard", n_shard)
    started = blank_after(conditions)
    heads_flat = once(heads_weight.reshape(feature_rows, 3 * width), started)
    if n_shard > 8 or n_ctx != 2:
        heads_rows = None
    else:
        heads_rows = swapped(heads_flat, "shard", n_shard)
    far = swap(
        once(jnp.concatenate([merge_weight, expand_weight, reduce_weight], axis=1), started),
        "tp", n_tp, 2,
    )
    merge_started = once(merge_weight, started)
    merge_near = swap(merge_started, "tp", n_tp, 1)
    merge_last = swap(merge_started, "tp", n_tp, 3)
    near_full = lax.all_gather(
        jnp.concatenate([expand_weight, reduce_weight], axis=1), owners, axis=0, tiled=True
    )
    silu_rows = jax.nn.silu(
        lax.dynamic_slice_in_dim(conditions, row_block * feature_rows, feature_rows, 1).astype(wide)
    ).astype(narrow)
    partial = product("ld,dkf->lkf", silu_rows, modulation_weight)
    local_modulation = scatter_small(partial, "shard", n_shard)
    local_modulation = add_all(local_modulation, "ctx", n_ctx) + modulation_bias.astype(wide)
    modulation = gather_small(local_modulation, "tp", n_tp)
    modulation = jnp.swapaxes(modulation, 0, 1).reshape(6, features)
    offset_one, scaling_one, gate_one, offset_two, scaling_two, gate_two = (
        modulation[k][None] for k in range(6)
    )
    issued = blank_after(local_modulation)
    if heads_rows is None:
        heads_pieces = [lax.all_gather(heads_flat, owners, axis=0, tiled=True)]
        spots = jnp.zeros((1,), jnp.int32)
    else:
        shard = lax.axis_index("shard")
        ctx = lax.axis_index("ctx")
        heads_other = [swap(once(rows, issued), "ctx", n_ctx, 1) for rows in heads_rows]
        heads_pieces = heads_rows + heads_other
        places = [(shard ^ k) * n_ctx for k in range(n_shard)]
        spots = jnp.stack([p + ctx for p in places] + [p + 1 - ctx for p in places])
    expand_biases = jnp.concatenate([expand_bias, swap(expand_bias, "tp", n_tp, 2)])[None]

    bias_rows = heads_bias.astype(wide)
    project_bias = jnp.concatenate([bias_rows[0], jnp.zeros_like(bias_rows[0]), bias_rows[1]])
    normed_one, queries, keys_here, values_here, heads_full = project(
        spots, latent, modulation, project_bias[None], heads_pieces
    )
    far_full = lax.all_gather(
        jnp.concatenate(
            [merge_weight, merge_near, far[:, :width], merge_last, far[:, width:]], axis=1
        )
        + blank_after(queries).astype(narrow),
        owners,
        axis=0,
        tiled=True,
    )
    keys = (keys_here, swap(keys_here, "ctx", n_ctx, 1))
    values = (values_here, swap(values_here, "ctx", n_ctx, 1))

    mixed_away, *kept_away = attend(1 - pair, group, queries, keys, values)
    mixed_near, *kept_near = attend(pair, group, queries, keys, values)
    across = swap(mixed_away, "tp", n_tp, 2)
    pieces = [mixed_near, swap(mixed_near, "tp", n_tp, 1), across, swap(across, "tp", n_tp, 1)]
    (
        branch_one,
        normed_two,
        branch_two_grad,
        activated,
        hidden_grad,
        hidden_bias_grad,
        branch_two_here,
        branch_two_there,
        grad_here,
        grad_there,
    ) = forward_back(
        jnp.stack([pair, side]),
        pieces,
        latent,
        cotangent[0],
        modulation,
        near_full,
        far_full,
        merge_bias[None],
        expand_biases,
    )
    arrived = swap(grad_there, "tp", n_tp, 1)
    middle, middle_grad, branch_one_grad, *mixture_grads, second_sums = middle_back(
        jnp.stack([tp_index, side]),
        latent,
        cotangent[0],
        branch_one,
        grad_here,
        arrived,
        modulation,
        far_full,
        width,
    )
    scattered = lax.psum_scatter(
        weight_grads(branch_two_grad, activated, normed_two, hidden_grad, min(512, hidden_width)),
        owners,
        scatter_dimension=0,
        tiled=True,
    )
    attended_grad = jnp.zeros((tokens, width), narrow)
    for k in range(n_tp):
        piece = swap(mixture_grads[k], "tp", n_tp, k) if k else mixture_grads[0]
        attended_grad = place(attended_grad, piece, tp_index ^ k)

    arrived_two = swap(once(branch_two_there, blank_after(mixture_grads[1])), "tp", n_tp, 1)
    branch_two = (
        branch_two_here.astype(wide)
        + arrived_two.astype(wide)
        + reduce_bias.astype(wide)
    )
    own_output = (middle + gate_two * branch_two).astype(narrow)
    output = gather_rows(own_output)
    gate_two_grad = jnp.sum(
        block_of(cotangent[0], tp_index, count).astype(wide) * branch_two, axis=0, keepdims=True
    )

    query_grad, key_grad_a, key_grad_b, value_grad_a, value_grad_b = attend_back(
        pair + zero_after(own_output), queries, attended_grad, kept_near, kept_away, keys, values
    )
    here, by_one, by_two, by_three, projected_grad, projected_sums, first_sums = project_back(
        jnp.stack([tp_index ^ k for k in range(n_tp)]),
        query_grad,
        key_grad_a,
        swap(key_grad_b, "ctx", n_ctx, 1),
        value_grad_a,
        swap(value_grad_b, "ctx", n_ctx, 1),
        latent,
        heads_full,
    )
    heads_bias_grad = jnp.concatenate(
        [projected_sums[0, :width], projected_sums[0, 2 * width :]]
    )
    beside = swap(by_three, "tp", n_tp, 1)
    far_sum = swap(
        (by_two.astype(wide) + beside.astype(wide)).astype(narrow), "tp", n_tp, 2
    )
    near_sum = swap(once(by_one, blank_after(beside)), "tp", n_tp, 1)
    own_mixture = jnp.concatenate([block_of(piece, side, count) for piece in pieces], axis=1)
    scattered_more = lax.psum_scatter(
        weight_grads(normed_one, projected_grad, branch_one_grad, own_mixture, width),
        owners,
        scatter_dimension=0,
        tiled=True,
    )
    heads_weight_grad = scattered_more[:, : 3 * width].astype(wide)
    merge_pieces = scattered_more[:, 3 * width :]
    reduce_near, reduce_far, expand_near, expand_far = (
        scattered[:, k * hidden_width : (k + 1) * hidden_width] for k in range(4)
    )
    far_pair = jnp.concatenate([reduce_far, expand_far], axis=1)
    both = swap(far_pair, "tp", n_tp, 2).astype(wide)
    reduce_weight_grad = reduce_near.astype(wide) + both[:, :hidden_width]
    expand_weight_grad = expand_near.astype(wide) + both[:, hidden_width:]
    merge_weight_grad = merge_pieces[:, :width].astype(wide)
    for k in range(1, n_tp):
        merge_weight_grad = merge_weight_grad + swap(
            merge_pieces[:, k * width : (k + 1) * width], "tp", n_tp, k
        ).astype(wide)
    expand_bias_grad = hidden_bias_grad[0, :hidden_width] + swap(
        hidden_bias_grad[0, hidden_width:], "tp", n_tp, 2
    )
    sums = jnp.concatenate([second_sums[:3], gate_two_grad, second_sums[3:5]], axis=0)
    first_sums = first_sums[:2]

    vectors = jnp.concatenate([first_sums, sums], axis=0)
    vectors = add_all(vectors, "tp", n_tp)
    local_grad = lax.dynamic_slice_in_dim(vectors[:6], tp_index * width, width, 1)
    common = jnp.concatenate(
        [
            local_grad.reshape(-1),
            vectors[6],
            vectors[7],
            expand_bias_grad,
            heads_bias_grad,
        ]
    )
    common = add_all(common, "ctx", n_ctx)
    local_grad = common[: 6 * width].reshape(6, width)
    biases = add_all(common[6 * width :], "shard", n_shard)
    modulation_grad = gather_small(local_grad, "shard", n_shard)
    modulation_bias_grad = jnp.sum(modulation_grad, axis=0)
    modulation_weight_grad = jnp.einsum(
        "ld,lkf->dkf", silu_rows.astype(wide), modulation_grad, precision=lax.Precision.HIGHEST
    )
    own_grad = latent_back(
        tp_index[None] + zero_after(modulation_weight_grad) + zero_after(far_pair),
        latent,
        middle_grad,
        modulation,
        (here, near_sum, far_sum),
    )
    latents_grad = gather_rows(own_grad).astype(wide)
    cuts = [features, features, hidden_width, 2 * width]
    edges = [sum(cuts[:k]) for k in range(len(cuts) + 1)]
    merge_bias_grad, reduce_bias_grad, expand_bias_grad, heads_bias_grad = (
        biases[edges[k] : edges[k + 1]] for k in range(4)
    )
    return (
        output[None],
        latents_grad[None],
        modulation_weight_grad,
        modulation_bias_grad,
        heads_weight_grad.reshape(feature_rows, 3, width),
        heads_bias_grad.reshape(2, width),
        merge_weight_grad,
        merge_bias_grad,
        expand_weight_grad,
        expand_bias_grad,
        reduce_weight_grad,
        reduce_bias_grad,
    )


def solution(mesh):
    sizes = tuple(mesh.shape[name] for name in ("shard", "ctx", "tp"))
    return jax.shard_map(
        functools.partial(body, sizes),
        mesh=mesh,
        in_specs=(
            P("shard", "ctx", None),
            P("shard", None),
            P(("shard", "ctx"), None, "tp"),
            P(None, "tp"),
            P(("shard", "ctx"), None, "tp"),
            P(None, "tp"),
            P(("shard", "ctx"), "tp"),
            P(),
            P(("shard", "ctx"), "tp"),
            P("tp"),
            P(("shard", "ctx"), "tp"),
            P(),
            P("shard", "ctx", None),
        ),
        out_specs=(
            P("shard", "ctx", None),
            P("shard", "ctx", None),
            P(("shard", "ctx"), None, "tp"),
            P(None, "tp"),
            P(("shard", "ctx"), None, "tp"),
            P(None, "tp"),
            P(("shard", "ctx"), "tp"),
            P(),
            P(("shard", "ctx"), "tp"),
            P("tp"),
            P(("shard", "ctx"), "tp"),
            P(),
        ),
        check_vma=False,
    )
```

```python
import functools
import math

import jax
import jax.numpy as jnp
from jax import lax
from jax.experimental import pallas as pl
from jax.experimental.pallas import tpu as pltpu
from jax.sharding import PartitionSpec as P

HD = 64


def swap(values, axis, size, distance):
    return lax.ppermute(values, axis, [(i, i ^ distance) for i in range(size)])


def swapped(values, axis, size):
    return [values] + [swap(values, axis, size, k) for k in range(1, size)]


def add_all(values, axis, size):
    step = 1
    while step < size:
        values = values + swap(values, axis, size, step)
        step *= 2
    return values


def gather_small(values, axis, size):
    if size > 8:
        return lax.all_gather(values, axis)
    pieces = swapped(values, axis, size)
    here = lax.axis_index(axis)
    rows = []
    for j in range(size):
        row = pieces[0]
        for k in range(1, size):
            row = jnp.where((here ^ j) == k, pieces[k], row)
        rows.append(row)
    return jnp.stack(rows)


def scatter_small(values, axis, size):
    if size > 8:
        return lax.psum_scatter(values, axis)
    here = lax.axis_index(axis)

    def piece(k):
        return lax.dynamic_index_in_dim(values, here ^ k, 0, keepdims=False)

    total = piece(0)
    for k in range(1, size):
        total = total + swap(piece(k), axis, size, k)
    return total


def zero_after(values):
    corner = lax.slice(values, (0,) * values.ndim, (1,) * values.ndim).reshape(())
    return (corner.astype(jnp.float32) * 0.0).astype(jnp.int32)


def blank_after(values):
    corner = lax.slice(values, (0,) * values.ndim, (1,) * values.ndim).reshape(())
    return corner.astype(jnp.float32) * 0.0


def block_of(values, index, count):
    return lax.dynamic_slice_in_dim(values, index * count, count, 0)


def place(whole, piece, index):
    return lax.dynamic_update_slice_in_dim(whole, piece, index * piece.shape[0], 0)


def spread(values):
    across = swap(values, "tp", 4, 2)
    return values, swap(values, "tp", 4, 1), across, swap(across, "tp", 4, 1)


def assembled(pieces, blank=0.0):
    here = lax.axis_index("tp")
    count = pieces[0].shape[0]
    whole = jnp.zeros((4 * count,) + pieces[0].shape[1:], pieces[0].dtype)
    whole = whole + jnp.asarray(blank).astype(whole.dtype)
    for k, piece in enumerate(pieces):
        whole = place(whole, piece, here ^ k)
    return whole


def normalise(values):
    centre = values - jnp.mean(values, axis=-1, keepdims=True)
    variance = jnp.mean(centre * centre, axis=-1, keepdims=True)
    scale = lax.rsqrt(variance + 1e-06)
    return centre * scale, scale


def normalise_back(grad, normed, scale):
    inner = grad - jnp.mean(grad, axis=-1, keepdims=True)
    return scale * (inner - normed * jnp.mean(grad * normed, axis=-1, keepdims=True))


def smooth_gate(values):
    return jax.nn.gelu(values, approximate=True)


def product(text, left, right):
    return jnp.einsum(text, left, right, preferred_element_type=jnp.float32)


def head_lanes(shape, head):
    lane = lax.broadcasted_iota(jnp.int32, shape, 1)
    return (lane >= head * HD) & (lane < (head + 1) * HD)


def dot(left, right, dims):
    return lax.dot_general(left, right, (dims, ((), ())), preferred_element_type=jnp.float32)


ROWS = ((1,), (1,))
PLAIN = ((1,), (0,))


def attend_kernel(spot, query, key_a, key_b, value_a, value_b, mixed, mixed_wide, log_total):
    queries = query[...] * jnp.asarray(HD ** (-0.5), jnp.bfloat16)
    gathered = jnp.zeros(mixed_wide.shape, jnp.float32)
    for head in range(queries.shape[1] // HD):
        lanes = head_lanes(queries.shape, head)
        own = jnp.where(lanes, queries, jnp.zeros_like(queries))
        score_a = dot(own, key_a[...], ROWS)
        score_b = dot(own, key_b[...], ROWS)
        top = jnp.maximum(
            jnp.max(score_a, axis=1, keepdims=True), jnp.max(score_b, axis=1, keepdims=True)
        )
        exp_a = jnp.exp(score_a - top)
        exp_b = jnp.exp(score_b - top)
        summed = jnp.sum(exp_a, axis=1, keepdims=True) + jnp.sum(exp_b, axis=1, keepdims=True)
        blend = dot(exp_a.astype(jnp.bfloat16), value_a[...], PLAIN)
        blend = blend + dot(exp_b.astype(jnp.bfloat16), value_b[...], PLAIN)
        gathered = jnp.where(lanes, blend / summed, gathered)
        log_total[:, head : head + 1] = top + jnp.log(summed)
    mixed[...] = gathered.astype(jnp.bfloat16)
    mixed_wide[...] = gathered


def attend(block, count, queries, keys, values):
    width = queries.shape[1]
    heads = width // HD
    tile = min(256, count)
    steps = count // tile

    def whole(array):
        return pl.BlockSpec(array.shape, lambda i, spot: (0, 0))

    def rows(columns):
        return pl.BlockSpec((tile, columns), lambda i, spot: (i, 0))

    return pl.pallas_call(
        attend_kernel,
        out_shape=(
            jax.ShapeDtypeStruct((count, width), jnp.bfloat16),
            jax.ShapeDtypeStruct((count, width), jnp.float32),
            jax.ShapeDtypeStruct((count, heads), jnp.float32),
        ),
        grid_spec=pltpu.PrefetchScalarGridSpec(
            num_scalar_prefetch=1,
            grid=(steps,),
            in_specs=[pl.BlockSpec((tile, width), lambda i, spot: (spot[0] * steps + i, 0))]
            + [whole(array) for array in (*keys, *values)],
            out_specs=(rows(width), rows(width), rows(heads)),
        ),
        compiler_params=pltpu.CompilerParams(vmem_limit_bytes=48 << 20),
        name="attend",
    )(block[None], queries, *keys, *values)


def attend_back_kernel(
    steps,
    spot, query, grad_a, grad_b, grad_c, grad_d, mixed_near, mixed_away, log_near, log_away,
    key_a, key_b, value_a, value_b,
    query_grad, key_grad_a, key_grad_b, value_grad_a, value_grad_b,
    key_sum_a, key_sum_b, value_sum_a, value_sum_b,
):
    @pl.when(pl.program_id(0) == 0)
    def _():
        for total in (key_sum_a, key_sum_b, value_sum_a, value_sum_b):
            total[...] = jnp.zeros(total.shape, jnp.float32)

    queries = query[...] * jnp.asarray(HD ** (-0.5), jnp.bfloat16)
    which = pl.program_id(0) ^ spot[1]
    upstream = grad_a[...]
    for k, grad in enumerate((grad_b, grad_c, grad_d)):
        upstream = jnp.where(which == k + 1, grad[...], upstream)
    is_near = pl.program_id(0) // (steps // 2) == spot[0]
    mixed = jnp.where(is_near, mixed_near[...], mixed_away[...])
    log_total = jnp.where(is_near, log_near[...], log_away[...])
    both = upstream.astype(jnp.float32) * mixed
    queries_flat = queries.T
    upstream_flat = upstream.T
    gathered = jnp.zeros(query_grad.shape, jnp.float32)
    blank = jnp.zeros_like(queries)
    for head in range(queries.shape[1] // HD):
        lanes = head_lanes(queries.shape, head)
        own = jnp.where(lanes, queries, blank)
        own_grad = jnp.where(lanes, upstream, blank)
        row_dot = jnp.sum(jnp.where(lanes, both, 0.0), axis=1, keepdims=True)
        total = log_total[:, head : head + 1]
        part = slice(head * HD, (head + 1) * HD)
        result = None
        for key, value, key_sum, value_sum in (
            (key_a, value_a, key_sum_a, value_sum_a),
            (key_b, value_b, key_sum_b, value_sum_b),
        ):
            scores = dot(own, key[...], ROWS)
            probs_grad = dot(own_grad, value[...], ROWS)
            weights = jnp.exp(scores - total)
            score_grad = (weights * (probs_grad - row_dot)).astype(jnp.bfloat16)
            attention = weights.astype(jnp.bfloat16)
            piece = dot(score_grad, key[...], PLAIN)
            result = piece if result is None else result + piece
            key_sum[part, :] += dot(queries_flat[part, :], score_grad, PLAIN)
            value_sum[part, :] += dot(upstream_flat[part, :], attention, PLAIN)
        gathered = jnp.where(lanes, result, gathered)
    query_grad[...] = (gathered * HD ** (-0.5)).astype(jnp.bfloat16)

    @pl.when(pl.program_id(0) == steps - 1)
    def _():
        key_grad_a[...] = key_sum_a[...].T
        value_grad_a[...] = value_sum_a[...].T
        key_grad_b[...] = key_sum_b[...].T.astype(jnp.bfloat16)
        value_grad_b[...] = value_sum_b[...].T.astype(jnp.bfloat16)


def attend_back(spots, queries, grads, near, away, keys, values):
    count, width = queries.shape
    heads = width // HD
    steps = len(grads)
    tile = count // steps
    tokens = keys[0].shape[0]

    def whole(array):
        return pl.BlockSpec(array.shape, lambda i, spot: (0, 0))

    def rows(columns):
        return pl.BlockSpec((tile, columns), lambda i, spot: (i, 0))

    def part(columns):
        return pl.BlockSpec((tile, columns), lambda i, spot: (i % (steps // 2), 0))

    high = jax.ShapeDtypeStruct((tokens, width), jnp.float32)
    low = jax.ShapeDtypeStruct((tokens, width), jnp.bfloat16)
    return pl.pallas_call(
        functools.partial(attend_back_kernel, steps),
        out_shape=(jax.ShapeDtypeStruct((count, width), jnp.bfloat16), high, low, high, low),
        grid_spec=pltpu.PrefetchScalarGridSpec(
            num_scalar_prefetch=1,
            grid=(steps,),
            in_specs=[
                rows(width),
                *[whole(grad) for grad in grads],
                part(width), part(width), part(heads), part(heads),
            ]
            + [whole(array) for array in (*keys, *values)],
            out_specs=(rows(width), whole(high), whole(low), whole(high), whole(low)),
            scratch_shapes=[pltpu.VMEM((width, tokens), jnp.float32) for _ in range(4)],
        ),
        compiler_params=pltpu.CompilerParams(vmem_limit_bytes=48 << 20),
        name="attend_back",
    )(spots, queries, *grads, near[0], away[0], near[1], away[1], *keys, *values)


def project_kernel(count, spots, latent, modulation, bias, *refs):
    pieces = refs[:count]
    normed, query, key, value, weight = refs[count:]
    width = query.shape[1]

    @pl.when(pl.program_id(0) == 0)
    def _():
        for k, piece in enumerate(pieces):
            size = piece.shape[0]
            weight[pl.ds(pl.multiple_of(spots[k] * size, size), size), :] = piece[...]

    rows = modulate_rows(
        latent[...].astype(jnp.float32), modulation[0:1, :], modulation[1:2, :]
    ).astype(jnp.bfloat16)
    normed[...] = rows
    flat = dot(rows, weight[...], PLAIN) + bias[...]
    query[...] = flat[:, :width].astype(jnp.bfloat16)
    key[...] = flat[:, width : 2 * width].astype(jnp.bfloat16)
    value[...] = flat[:, 2 * width :].astype(jnp.bfloat16)


def project(spots, latent, modulation, bias, pieces):
    tokens, features = latent.shape
    columns = bias.shape[1]
    width = columns // 3
    tile = min(256, tokens)

    def still(shape):
        return pl.BlockSpec(shape, lambda i, spots: (0, 0))

    def moving(size):
        return pl.BlockSpec((tile, size), lambda i, spots: (i, 0))

    def low(*shape):
        return jax.ShapeDtypeStruct(shape, jnp.bfloat16)

    return pl.pallas_call(
        functools.partial(project_kernel, len(pieces)),
        out_shape=(
            low(tokens, features),
            low(tokens, width),
            low(tokens, width),
            low(tokens, width),
            low(features, columns),
        ),
        grid_spec=pltpu.PrefetchScalarGridSpec(
            num_scalar_prefetch=1,
            grid=(tokens // tile,),
            in_specs=[moving(features), still(modulation.shape), still(bias.shape)]
            + [still(piece.shape) for piece in pieces],
            out_specs=(
                moving(features),
                moving(width),
                moving(width),
                moving(width),
                still((features, columns)),
            ),
        ),
        compiler_params=pltpu.CompilerParams(vmem_limit_bytes=48 << 20),
        name="project",
    )(spots, latent, modulation, bias, *pieces)


def project_back_kernel(
    spots, query, key_a, key_b, value_a, value_b, latent, weight,
    grad_a, grad_b, grad_c, grad_d, joined, sums, token_sums,
):
    @pl.when(pl.program_id(0) == 0)
    def _():
        sums[...] = jnp.zeros(sums.shape, jnp.float32)
        token_sums[...] = jnp.zeros(token_sums.shape, jnp.float32)

    flat = jnp.concatenate(
        [
            query[...],
            (key_a[...] + key_b[...].astype(jnp.float32)).astype(jnp.bfloat16),
            (value_a[...] + value_b[...].astype(jnp.float32)).astype(jnp.bfloat16),
        ],
        axis=1,
    )
    joined[...] = flat
    sums[...] += jnp.sum(flat.astype(jnp.float32), axis=0, keepdims=True)
    result = dot(flat, weight[...], ROWS)
    normed = normalise(latent[...].astype(jnp.float32))[0]
    token_sums[0:1, :] += row_sum(result)
    token_sums[1:2, :] += row_sum(result * normed)
    result = result.astype(jnp.bfloat16)
    for k, grad in enumerate((grad_a, grad_b, grad_c, grad_d)):

        @pl.when(pl.program_id(0) == k)
        def _(grad=grad):
            grad[...] = result


def project_back(spots, query, key_a, key_b, value_a, value_b, latent, weight):
    tokens, width = query.shape
    features, columns = weight.shape
    tile = tokens // 4

    def moving(size):
        return pl.BlockSpec((tile, size), lambda i, spots: (spots[i], 0))

    def still(shape):
        return pl.BlockSpec(shape, lambda i, spots: (0, 0))

    piece = jax.ShapeDtypeStruct((tile, features), jnp.bfloat16)
    return pl.pallas_call(
        project_back_kernel,
        out_shape=(
            piece,
            piece,
            piece,
            piece,
            jax.ShapeDtypeStruct((tokens, columns), jnp.bfloat16),
            jax.ShapeDtypeStruct((1, columns), jnp.float32),
            jax.ShapeDtypeStruct((8, features), jnp.float32),
        ),
        grid_spec=pltpu.PrefetchScalarGridSpec(
            num_scalar_prefetch=1,
            grid=(4,),
            in_specs=[moving(width)] * 5 + [moving(features), still(weight.shape)],
            out_specs=(still(piece.shape),) * 4
            + (moving(columns), still((1, columns)), still((8, features))),
        ),
        compiler_params=pltpu.CompilerParams(vmem_limit_bytes=48 << 20),
        name="project_back",
    )(spots, query, key_a, key_b, value_a, value_b, latent, weight)


def row_sum(values):
    return jnp.sum(values, axis=0, keepdims=True)


def middle_back_kernel(
    spots, latent, cotangent, branch_one, grad_here, grad_there, modulation, merge,
    middle, middle_grad, branch_one_grad, piece_a, piece_b, piece_c, piece_d, sums,
):
    branch = branch_one[...]
    upstream = cotangent[...].astype(jnp.float32)
    centre = latent[...].astype(jnp.float32) + modulation[2:3, :] * branch
    middle[...] = centre
    normed, scale = normalise(centre)
    grad = grad_here[...].astype(jnp.float32) + grad_there[...].astype(jnp.float32)
    total = upstream + normalise_back(grad * (1.0 + modulation[4:5, :]), normed, scale)
    middle_grad[...] = total
    branch_grad = (modulation[2:3, :] * total).astype(jnp.bfloat16)
    branch_one_grad[...] = branch_grad
    mixed = dot(branch_grad, merge[...], PLAIN).astype(jnp.bfloat16)
    width = piece_a.shape[1]
    for k, piece in enumerate((piece_a, piece_b, piece_c, piece_d)):
        piece[...] = mixed[:, k * width : (k + 1) * width]
    scaled = (modulation[5:6, :] * upstream).astype(jnp.bfloat16).astype(jnp.float32)
    sums[0:1, :] = row_sum(total * branch)
    sums[1:2, :] = row_sum(grad)
    sums[2:3, :] = row_sum(grad * normed)
    sums[3:4, :] = row_sum(branch_grad.astype(jnp.float32))
    sums[4:5, :] = row_sum(scaled)
    sums[5:8, :] = jnp.zeros((3, sums.shape[1]), jnp.float32)


def middle_back(spots, latent, cotangent, branch_one, here, there, modulation, far, width):
    count, features = here.shape

    def still(shape):
        return pl.BlockSpec(shape, lambda i, spots: (0, 0))

    def picked(place_at):
        return pl.BlockSpec((count, features), lambda i, spots: (spots[place_at], 0))

    def low(*shape):
        return jax.ShapeDtypeStruct(shape, jnp.bfloat16)

    def high(*shape):
        return jax.ShapeDtypeStruct(shape, jnp.float32)

    shapes = (
        high(count, features),
        high(count, features),
        low(count, features),
        low(count, width),
        low(count, width),
        low(count, width),
        low(count, width),
        high(8, features),
    )
    return pl.pallas_call(
        middle_back_kernel,
        out_shape=shapes,
        grid_spec=pltpu.PrefetchScalarGridSpec(
            num_scalar_prefetch=1,
            grid=(1,),
            in_specs=[
                picked(0),
                picked(0),
                picked(1),
                still(here.shape),
                still(there.shape),
                still(modulation.shape),
                still((features, features)),
            ],
            out_specs=tuple(still(shape.shape) for shape in shapes),
        ),
        compiler_params=pltpu.CompilerParams(vmem_limit_bytes=48 << 20),
        name="middle_back",
    )(spots, latent, cotangent, branch_one, here, there, modulation, far)


def latent_back_kernel(spots, latent, middle_grad, modulation, part_a, part_b, part_c, result):
    normed, scale = normalise(latent[...].astype(jnp.float32))
    grad = (
        part_a[...].astype(jnp.float32)
        + part_b[...].astype(jnp.float32)
        + part_c[...].astype(jnp.float32)
    )
    total = middle_grad[...] + normalise_back(grad * (1.0 + modulation[1:2, :]), normed, scale)
    result[...] = total.astype(jnp.bfloat16)


def latent_back(spots, latent, middle_grad, modulation, parts):
    count, features = middle_grad.shape

    def still(shape):
        return pl.BlockSpec(shape, lambda i, spots: (0, 0))

    square = still((count, features))
    return pl.pallas_call(
        latent_back_kernel,
        out_shape=jax.ShapeDtypeStruct((count, features), jnp.bfloat16),
        grid_spec=pltpu.PrefetchScalarGridSpec(
            num_scalar_prefetch=1,
            grid=(1,),
            in_specs=[
                pl.BlockSpec((count, features), lambda i, spots: (spots[0], 0)),
                square,
                still(modulation.shape),
                square,
                square,
                square,
            ],
            out_specs=square,
        ),
        compiler_params=pltpu.CompilerParams(vmem_limit_bytes=48 << 20),
        name="latent_back",
    )(spots, latent, middle_grad, modulation, *parts)


def modulate_rows(values, offset, scaling):
    return normalise(values)[0] * (1.0 + scaling) + offset


def smooth_gate_both(values):
    cubic = math.sqrt(2.0 / math.pi) * (values + 0.044715 * values * values * values)
    slope = math.sqrt(2.0 / math.pi) * (1.0 + 3.0 * 0.044715 * values * values)
    bend = jnp.tanh(cubic)
    lifted = 0.5 * (1.0 + bend)
    return values * lifted, lifted + 0.5 * values * (1.0 - bend * bend) * slope


def forward_back_kernel(
    steps,
    spot,
    piece_a, piece_b, piece_c, piece_d,
    latent, cotangent, modulation, merge, merge_bias,
    expand_near, expand_far, reduce_near, reduce_far, bias,
    branch_one, normed_two, branch_two_grad, activated, hidden_grad, bias_grad,
    branch_two_here, branch_two_there, grad_here, grad_there,
    forward_sum, backward_sum,
):
    step = pl.program_id(0)

    @pl.when(step == 0)
    def _():
        mixture = jnp.concatenate(
            [piece_a[...], piece_b[...], piece_c[...], piece_d[...]], axis=1
        )
        branch = dot(mixture, merge[...], ROWS) + merge_bias[...].astype(jnp.float32)
        branch_one[...] = branch
        middle = latent[...].astype(jnp.float32) + modulation[2:3, :] * branch
        normed_two[...] = modulate_rows(
            middle, modulation[3:4, :], modulation[4:5, :]
        ).astype(jnp.bfloat16)
        branch_two_grad[...] = (
            modulation[5:6, :] * cotangent[...].astype(jnp.float32)
        ).astype(jnp.bfloat16)
        forward_sum[...] = jnp.zeros(forward_sum.shape, jnp.float32)
        backward_sum[...] = jnp.zeros(backward_sum.shape, jnp.float32)

    def block(expand, reduce):
        hidden = dot(normed_two[...], expand[...], PLAIN) + bias[...].astype(jnp.float32)
        value, slope = smooth_gate_both(hidden)
        value = value.astype(jnp.bfloat16)
        activated[...] = value
        grad = dot(branch_two_grad[...], reduce[...], PLAIN) * slope
        grad = grad.astype(jnp.bfloat16)
        hidden_grad[...] = grad
        bias_grad[...] = jnp.sum(grad.astype(jnp.float32), axis=0, keepdims=True)
        backward_sum[...] += dot(grad, expand[...], ROWS)
        forward_sum[...] += dot(value, reduce[...], ROWS)

    @pl.when(step < steps // 2)
    def _():
        block(expand_near, reduce_near)

    @pl.when(step >= steps // 2)
    def _():
        block(expand_far, reduce_far)

    @pl.when(step == steps - 1)
    def _():
        count = grad_here.shape[0]
        here = pl.ds(pl.multiple_of(spot[1] * count, count), count)
        there = pl.ds(pl.multiple_of((1 - spot[1]) * count, count), count)
        branch_two_here[...] = forward_sum[here, :].astype(jnp.bfloat16)
        branch_two_there[...] = forward_sum[there, :].astype(jnp.bfloat16)
        grad_here[...] = backward_sum[here, :].astype(jnp.bfloat16)
        grad_there[...] = backward_sum[there, :].astype(jnp.bfloat16)


def forward_back(spots, pieces, latent, cotangent, modulation, near, far, merge_bias, bias):
    rows, width = pieces[0].shape
    features = latent.shape[1]
    hidden = bias.shape[1] // 2
    tile = min(512, hidden)
    per = hidden // tile
    steps = 2 * per
    ahead = features // tile

    def still(array):
        return pl.BlockSpec(array.shape, lambda j, spot: (0, 0))

    def picked():
        return pl.BlockSpec((rows, features), lambda j, spot: (spot[0], 0))

    def column(first, lag):
        def place_at(j, spot):
            return (0, first + jnp.clip(j - lag, 0, per - 1))

        return pl.BlockSpec((features, tile), place_at)

    moving = pl.BlockSpec((rows, tile), lambda j, spot: (0, j))
    row_tile = pl.BlockSpec((1, tile), lambda j, spot: (0, j))
    square = pl.BlockSpec((rows, features), lambda j, spot: (0, 0))
    piece = pl.BlockSpec((rows // 2, features), lambda j, spot: (0, 0))
    low = jax.ShapeDtypeStruct((rows, features), jnp.bfloat16)
    high = jax.ShapeDtypeStruct((rows, features), jnp.float32)
    lower = jax.ShapeDtypeStruct((rows // 2, features), jnp.bfloat16)
    return pl.pallas_call(
        functools.partial(forward_back_kernel, steps),
        out_shape=(
            high,
            low,
            low,
            jax.ShapeDtypeStruct((rows, 2 * hidden), jnp.bfloat16),
            jax.ShapeDtypeStruct((rows, 2 * hidden), jnp.bfloat16),
            jax.ShapeDtypeStruct((1, 2 * hidden), jnp.float32),
            lower,
            lower,
            lower,
            lower,
        ),
        grid_spec=pltpu.PrefetchScalarGridSpec(
            num_scalar_prefetch=1,
            grid=(steps,),
            in_specs=[still(piece) for piece in pieces]
            + [
                picked(),
                picked(),
                still(modulation),
                pl.BlockSpec((features, features), lambda j, spot: (0, 0)),
                still(merge_bias),
                column(0, 0),
                column(ahead, per),
                column(per, 0),
                column(ahead + per, per),
                row_tile,
            ],
            out_specs=(square, square, square, moving, moving, row_tile, piece, piece, piece, piece),
            scratch_shapes=[
                pltpu.VMEM((rows, features), jnp.float32),
                pltpu.VMEM((rows, features), jnp.float32),
            ],
        ),
        compiler_params=pltpu.CompilerParams(vmem_limit_bytes=58 << 20),
        name="forward_back",
    )(spots, *pieces, latent, cotangent, modulation, far, merge_bias, near, far, near, far, bias)


def weight_grad_kernel(
    per, waited, first_left, first_right, second_left, second_right, result, turned, turned_second
):
    step = pl.program_id(0)

    @pl.when(step == 0)
    def _():
        turned[...] = first_left[...].T

    @pl.when(step == per)
    def _():
        turned_second[...] = second_left[...].T

    @pl.when(step < per)
    def _():
        result[...] = dot(turned[...], first_right[...], PLAIN).astype(jnp.bfloat16)

    @pl.when(step >= per)
    def _():
        result[...] = dot(turned_second[...], second_right[...], PLAIN).astype(jnp.bfloat16)


def weight_grads(waited, first_left, first_right, second_left, second_right, tile):
    features = first_left.shape[1]
    per = first_right.shape[1] // tile
    more = second_right.shape[1] // tile

    def still(array):
        return pl.BlockSpec(array.shape, lambda j, waited: (0, 0))

    return pl.pallas_call(
        functools.partial(weight_grad_kernel, per),
        out_shape=jax.ShapeDtypeStruct((features, (per + more) * tile), jnp.bfloat16),
        grid_spec=pltpu.PrefetchScalarGridSpec(
        num_scalar_prefetch=1,
        grid=(per + more,),
        in_specs=[
            still(first_left),
            pl.BlockSpec((first_right.shape[0], tile), lambda j, waited: (0, jnp.minimum(j, per - 1))),
            still(second_left),
            pl.BlockSpec((second_right.shape[0], tile), lambda j, waited: (0, jnp.maximum(j - per, 0))),
        ],
        out_specs=pl.BlockSpec((features, tile), lambda j, waited: (0, j)),
        scratch_shapes=[
            pltpu.VMEM((features, first_left.shape[0]), jnp.bfloat16),
            pltpu.VMEM((features, second_left.shape[0]), jnp.bfloat16),
        ],
        ),
        compiler_params=pltpu.CompilerParams(vmem_limit_bytes=48 << 20),
        name="weight_grads",
    )(waited[None], first_left, first_right, second_left, second_right)


def body(
    sizes,
    latents,
    condition,
    modulation_weight,
    modulation_bias,
    heads_weight,
    heads_bias,
    merge_weight,
    merge_bias,
    expand_weight,
    expand_bias,
    reduce_weight,
    reduce_bias,
    cotangent,
):
    n_shard, n_ctx, n_tp = sizes
    if n_tp != 4 or latents.shape[0] != 1:
        raise ValueError("unsupported split")
    wide = jnp.float32
    narrow = jnp.bfloat16
    owners = ("shard", "ctx")
    row_block = lax.axis_index("shard") * n_ctx + lax.axis_index("ctx")
    tp_index = lax.axis_index("tp")
    pair = tp_index // 2
    side = tp_index % 2
    feature_rows = modulation_weight.shape[0]
    width = modulation_weight.shape[2]
    hidden_width = expand_weight.shape[1]
    latent = latents[0]
    tokens, features = latent.shape
    group = tokens // 2
    count = tokens // n_tp

    def once(values, token):
        return values + token.astype(values.dtype)

    conditions = gather_small(condition[0], "shard", n_shard)
    started = blank_after(conditions)
    heads_flat = once(heads_weight.reshape(feature_rows, 3 * width), started)
    if n_shard > 8 or n_ctx != 2:
        heads_rows = None
    else:
        heads_rows = swapped(heads_flat, "shard", n_shard)
    near_full = lax.all_gather(
        jnp.concatenate([expand_weight, reduce_weight], axis=1), owners, axis=0, tiled=True
    )
    silu_rows = jax.nn.silu(
        lax.dynamic_slice_in_dim(conditions, row_block * feature_rows, feature_rows, 1).astype(wide)
    ).astype(narrow)
    partial = product("ld,dkf->lkf", silu_rows, modulation_weight)
    local_modulation = scatter_small(partial, "shard", n_shard)
    local_modulation = add_all(local_modulation, "ctx", n_ctx) + modulation_bias.astype(wide)
    bias_away = swap(expand_bias, "tp", n_tp, 2)
    for early in [bias_away] + (heads_rows or [])[1:]:
        local_modulation = local_modulation + blank_after(early)
    modulation = gather_small(local_modulation, "tp", n_tp)
    modulation = jnp.swapaxes(modulation, 0, 1).reshape(6, features)
    offset_one, scaling_one, gate_one, offset_two, scaling_two, gate_two = (
        modulation[k][None] for k in range(6)
    )
    issued = blank_after(local_modulation)
    settled = blank_after(modulation)
    far = swap(
        once(jnp.concatenate([merge_weight, expand_weight, reduce_weight], axis=1), settled),
        "tp", n_tp, 2,
    )
    merge_settled = once(merge_weight, settled)
    merge_near = swap(merge_settled, "tp", n_tp, 1)
    merge_last = swap(merge_settled, "tp", n_tp, 3)
    far_rows = jnp.concatenate(
        [merge_weight, merge_near, far[:, :width], merge_last, far[:, width:]], axis=1
    )
    far_full = lax.all_gather(far_rows, owners, axis=0, tiled=True)
    if heads_rows is None:
        heads_pieces = [lax.all_gather(heads_flat, owners, axis=0, tiled=True)]
        spots = jnp.zeros((1,), jnp.int32)
    else:
        shard = lax.axis_index("shard")
        ctx = lax.axis_index("ctx")
        heads_other = [swap(once(rows, issued), "ctx", n_ctx, 1) for rows in heads_rows]
        heads_pieces = heads_rows + heads_other
        places = [(shard ^ k) * n_ctx for k in range(n_shard)]
        spots = jnp.stack([p + ctx for p in places] + [p + 1 - ctx for p in places])
    expand_biases = jnp.concatenate([expand_bias, bias_away])[None]

    bias_rows = heads_bias.astype(wide)
    project_bias = jnp.concatenate([bias_rows[0], jnp.zeros_like(bias_rows[0]), bias_rows[1]])
    normed_one, queries, keys_here, values_here, heads_full = project(
        spots + zero_after(far_rows), latent, modulation, project_bias[None], heads_pieces
    )
    keys = (keys_here, swap(keys_here, "ctx", n_ctx, 1))
    values = (values_here, swap(values_here, "ctx", n_ctx, 1))

    mixed_away, *kept_away = attend(1 - pair, group, queries, keys, values)
    mixed_near, *kept_near = attend(pair, group, queries, keys, values)
    across = swap(mixed_away, "tp", n_tp, 2)
    pieces = [mixed_near, swap(mixed_near, "tp", n_tp, 1), across, swap(across, "tp", n_tp, 1)]
    (
        branch_one,
        normed_two,
        branch_two_grad,
        activated,
        hidden_grad,
        hidden_bias_grad,
        branch_two_here,
        branch_two_there,
        grad_here,
        grad_there,
    ) = forward_back(
        jnp.stack([pair, side]),
        pieces,
        latent,
        cotangent[0],
        modulation,
        near_full,
        far_full,
        merge_bias[None],
        expand_biases,
    )
    arrived = swap(grad_there, "tp", n_tp, 1)
    hidden_grads = weight_grads(
        jnp.int32(0), branch_two_grad, activated, normed_two, hidden_grad, min(512, hidden_width)
    )
    middle, middle_grad, branch_one_grad, *mixture_grads, second_sums = middle_back(
        jnp.stack([tp_index, side]) + zero_after(hidden_grads),
        latent,
        cotangent[0],
        branch_one,
        grad_here,
        arrived,
        modulation,
        far_full,
        width,
    )
    received = [
        swap(mixture_grads[k], "tp", n_tp, k) if k else mixture_grads[0] for k in range(n_tp)
    ]
    scattered = lax.psum_scatter(
        hidden_grads,
        owners,
        scatter_dimension=0,
        tiled=True,
    )

    arrived_two = swap(branch_two_there, "tp", n_tp, 1)
    branch_two = (
        branch_two_here.astype(wide)
        + arrived_two.astype(wide)
        + reduce_bias.astype(wide)
    )
    own_output = (middle + gate_two * branch_two).astype(narrow)
    output_pieces = spread(own_output)
    output = assembled(output_pieces)
    gate_two_grad = jnp.sum(
        block_of(cotangent[0], tp_index, count).astype(wide) * branch_two, axis=0, keepdims=True
    )

    query_grad, key_grad_a, key_grad_b, value_grad_a, value_grad_b = attend_back(
        jnp.stack([pair, tp_index]), queries, received, kept_near, kept_away, keys, values
    )
    here, by_one, by_two, by_three, projected_grad, projected_sums, first_sums = project_back(
        jnp.stack([tp_index ^ k for k in range(n_tp)])
        + zero_after(output_pieces[1])
        + zero_after(output_pieces[2]),
        query_grad,
        key_grad_a,
        swap(key_grad_b, "ctx", n_ctx, 1),
        value_grad_a,
        swap(value_grad_b, "ctx", n_ctx, 1),
        latent,
        heads_full,
    )
    heads_bias_grad = jnp.concatenate(
        [projected_sums[0, :width], projected_sums[0, 2 * width :]]
    )
    beside = swap(by_three, "tp", n_tp, 1)
    from_far = [
        swap((by_two.astype(wide) + beside.astype(wide)).astype(narrow), "tp", n_tp, 2)
    ]
    near_sum = swap(once(by_one, blank_after(beside)), "tp", n_tp, 1)
    own_mixture = jnp.concatenate([block_of(piece, side, count) for piece in pieces], axis=1)
    scattered_more = lax.psum_scatter(
        weight_grads(
            zero_after(scattered) + zero_after(beside), normed_one, projected_grad, branch_one_grad, own_mixture, width),
        owners,
        scatter_dimension=0,
        tiled=True,
    )
    heads_weight_grad = scattered_more[:, : 3 * width].astype(wide)
    merge_pieces = scattered_more[:, 3 * width :]
    reduce_near, reduce_far, expand_near, expand_far = (
        scattered[:, k * hidden_width : (k + 1) * hidden_width] for k in range(4)
    )
    far_pair = jnp.concatenate([reduce_far, expand_far], axis=1)
    both = swap(far_pair, "tp", n_tp, 2).astype(wide)
    reduce_weight_grad = reduce_near.astype(wide) + both[:, :hidden_width]
    expand_weight_grad = expand_near.astype(wide) + both[:, hidden_width:]
    merge_weight_grad = merge_pieces[:, :width].astype(wide)
    for k in range(1, n_tp):
        merge_weight_grad = merge_weight_grad + swap(
            merge_pieces[:, k * width : (k + 1) * width], "tp", n_tp, k
        ).astype(wide)
    expand_bias_grad = hidden_bias_grad[0, :hidden_width] + swap(
        hidden_bias_grad[0, hidden_width:], "tp", n_tp, 2
    )
    sums = jnp.concatenate([second_sums[:3], gate_two_grad, second_sums[3:5]], axis=0)
    first_sums = first_sums[:2]

    own_grad = latent_back(
        tp_index[None],
        latent,
        middle_grad,
        modulation,
        (here, near_sum, *from_far),
    )
    vectors = jnp.concatenate([first_sums, sums], axis=0) + blank_after(own_grad)
    vectors = add_all(vectors, "tp", n_tp)
    local_grad = lax.dynamic_slice_in_dim(vectors[:6], tp_index * width, width, 1)
    common = jnp.concatenate(
        [
            local_grad.reshape(-1),
            vectors[6],
            vectors[7],
            expand_bias_grad,
            heads_bias_grad,
        ]
    )
    common = add_all(common, "ctx", n_ctx)
    local_grad = common[: 6 * width].reshape(6, width)
    biases = add_all(common[6 * width :], "shard", n_shard)
    modulation_grad = gather_small(local_grad, "shard", n_shard)
    modulation_bias_grad = jnp.sum(modulation_grad, axis=0)
    modulation_weight_grad = jnp.einsum(
        "ld,lkf->dkf", silu_rows.astype(wide), modulation_grad, precision=lax.Precision.HIGHEST
    )
    latents_grad = assembled(spread(own_grad)).astype(wide)
    cuts = [features, features, hidden_width, 2 * width]
    edges = [sum(cuts[:k]) for k in range(len(cuts) + 1)]
    merge_bias_grad, reduce_bias_grad, expand_bias_grad, heads_bias_grad = (
        biases[edges[k] : edges[k + 1]] for k in range(4)
    )
    return (
        output[None],
        latents_grad[None],
        modulation_weight_grad,
        modulation_bias_grad,
        heads_weight_grad.reshape(feature_rows, 3, width),
        heads_bias_grad.reshape(2, width),
        merge_weight_grad,
        merge_bias_grad,
        expand_weight_grad,
        expand_bias_grad,
        reduce_weight_grad,
        reduce_bias_grad,
    )


def solution(mesh):
    sizes = tuple(mesh.shape[name] for name in ("shard", "ctx", "tp"))
    return jax.shard_map(
        functools.partial(body, sizes),
        mesh=mesh,
        in_specs=(
            P("shard", "ctx", None),
            P("shard", None),
            P(("shard", "ctx"), None, "tp"),
            P(None, "tp"),
            P(("shard", "ctx"), None, "tp"),
            P(None, "tp"),
            P(("shard", "ctx"), "tp"),
            P(),
            P(("shard", "ctx"), "tp"),
            P("tp"),
            P(("shard", "ctx"), "tp"),
            P(),
            P("shard", "ctx", None),
        ),
        out_specs=(
            P("shard", "ctx", None),
            P("shard", "ctx", None),
            P(("shard", "ctx"), None, "tp"),
            P(None, "tp"),
            P(("shard", "ctx"), None, "tp"),
            P(None, "tp"),
            P(("shard", "ctx"), "tp"),
            P(),
            P(("shard", "ctx"), "tp"),
            P("tp"),
            P(("shard", "ctx"), "tp"),
            P(),
        ),
        check_vma=False,
    )
```

```python
import functools
import math

import jax
import jax.numpy as jnp
from jax import lax
from jax.experimental import pallas as pl
from jax.experimental.pallas import tpu as pltpu
from jax.sharding import PartitionSpec as P

HD = 64


def swap(values, axis, size, distance):
    return lax.ppermute(values, axis, [(i, i ^ distance) for i in range(size)])


def swapped(values, axis, size):
    return [values] + [swap(values, axis, size, k) for k in range(1, size)]


def add_all(values, axis, size):
    step = 1
    while step < size:
        values = values + swap(values, axis, size, step)
        step *= 2
    return values


def gather_small(values, axis, size):
    if size > 8:
        return lax.all_gather(values, axis)
    pieces = swapped(values, axis, size)
    here = lax.axis_index(axis)
    rows = []
    for j in range(size):
        row = pieces[0]
        for k in range(1, size):
            row = jnp.where((here ^ j) == k, pieces[k], row)
        rows.append(row)
    return jnp.stack(rows)


def scatter_small(values, axis, size):
    if size > 8:
        return lax.psum_scatter(values, axis)
    here = lax.axis_index(axis)

    def piece(k):
        return lax.dynamic_index_in_dim(values, here ^ k, 0, keepdims=False)

    total = piece(0)
    for k in range(1, size):
        total = total + swap(piece(k), axis, size, k)
    return total


def zero_after(values):
    corner = lax.slice(values, (0,) * values.ndim, (1,) * values.ndim).reshape(())
    return (corner.astype(jnp.float32) * 0.0).astype(jnp.int32)


def blank_after(values):
    corner = lax.slice(values, (0,) * values.ndim, (1,) * values.ndim).reshape(())
    return corner.astype(jnp.float32) * 0.0


def block_of(values, index, count):
    return lax.dynamic_slice_in_dim(values, index * count, count, 0)


def place(whole, piece, index):
    return lax.dynamic_update_slice_in_dim(whole, piece, index * piece.shape[0], 0)


def spread(values):
    across = swap(values, "tp", 4, 2)
    return values, swap(values, "tp", 4, 1), across, swap(across, "tp", 4, 1)


def assembled(pieces, blank=0.0):
    here = lax.axis_index("tp")
    count = pieces[0].shape[0]
    whole = jnp.zeros((4 * count,) + pieces[0].shape[1:], pieces[0].dtype)
    whole = whole + jnp.asarray(blank).astype(whole.dtype)
    for k, piece in enumerate(pieces):
        whole = place(whole, piece, here ^ k)
    return whole


def normalise(values):
    centre = values - jnp.mean(values, axis=-1, keepdims=True)
    variance = jnp.mean(centre * centre, axis=-1, keepdims=True)
    scale = lax.rsqrt(variance + 1e-06)
    return centre * scale, scale


def normalise_back(grad, normed, scale):
    inner = grad - jnp.mean(grad, axis=-1, keepdims=True)
    return scale * (inner - normed * jnp.mean(grad * normed, axis=-1, keepdims=True))


def smooth_gate(values):
    return jax.nn.gelu(values, approximate=True)


def product(text, left, right):
    return jnp.einsum(text, left, right, preferred_element_type=jnp.float32)


def after(count, kernel):
    def run(spot, *refs):
        kernel(spot, *refs[count:])

    return run


def held(arrays):
    return [pl.BlockSpec(memory_space=pl.ANY) for _ in arrays]


def head_lanes(shape, head):
    lane = lax.broadcasted_iota(jnp.int32, shape, 1)
    return (lane >= head * HD) & (lane < (head + 1) * HD)


def dot(left, right, dims):
    return lax.dot_general(left, right, (dims, ((), ())), preferred_element_type=jnp.float32)


ROWS = ((1,), (1,))
PLAIN = ((1,), (0,))


def attend_kernel(spot, query, key_a, key_b, value_a, value_b, mixed, mixed_wide, log_total):
    queries = query[...] * jnp.asarray(HD ** (-0.5), jnp.bfloat16)
    gathered = jnp.zeros(mixed_wide.shape, jnp.float32)
    for head in range(queries.shape[1] // HD):
        lanes = head_lanes(queries.shape, head)
        own = jnp.where(lanes, queries, jnp.zeros_like(queries))
        score_a = dot(own, key_a[...], ROWS)
        score_b = dot(own, key_b[...], ROWS)
        top = jnp.maximum(
            jnp.max(score_a, axis=1, keepdims=True), jnp.max(score_b, axis=1, keepdims=True)
        )
        exp_a = jnp.exp(score_a - top)
        exp_b = jnp.exp(score_b - top)
        summed = jnp.sum(exp_a, axis=1, keepdims=True) + jnp.sum(exp_b, axis=1, keepdims=True)
        blend = dot(exp_a.astype(jnp.bfloat16), value_a[...], PLAIN)
        blend = blend + dot(exp_b.astype(jnp.bfloat16), value_b[...], PLAIN)
        gathered = jnp.where(lanes, blend / summed, gathered)
        log_total[:, head : head + 1] = top + jnp.log(summed)
    mixed[...] = gathered.astype(jnp.bfloat16)
    mixed_wide[...] = gathered


def attend(block, count, queries, keys, values):
    width = queries.shape[1]
    heads = width // HD
    tile = min(256, count)
    steps = count // tile

    def whole(array):
        return pl.BlockSpec(array.shape, lambda i, spot: (0, 0))

    def rows(columns):
        return pl.BlockSpec((tile, columns), lambda i, spot: (i, 0))

    return pl.pallas_call(
        attend_kernel,
        out_shape=(
            jax.ShapeDtypeStruct((count, width), jnp.bfloat16),
            jax.ShapeDtypeStruct((count, width), jnp.float32),
            jax.ShapeDtypeStruct((count, heads), jnp.float32),
        ),
        grid_spec=pltpu.PrefetchScalarGridSpec(
            num_scalar_prefetch=1,
            grid=(steps,),
            in_specs=[pl.BlockSpec((tile, width), lambda i, spot: (spot[0] * steps + i, 0))]
            + [whole(array) for array in (*keys, *values)],
            out_specs=(rows(width), rows(width), rows(heads)),
        ),
        compiler_params=pltpu.CompilerParams(vmem_limit_bytes=48 << 20),
        name="attend",
    )(block[None], queries, *keys, *values)


def attend_back_kernel(
    steps,
    spot, query, grad_a, grad_b, grad_c, grad_d, mixed_near, mixed_away, log_near, log_away,
    key_a, key_b, value_a, value_b,
    query_grad, key_grad_a, key_grad_b, value_grad_a, value_grad_b,
    key_sum_a, key_sum_b, value_sum_a, value_sum_b,
):
    @pl.when(pl.program_id(0) == 0)
    def _():
        for total in (key_sum_a, key_sum_b, value_sum_a, value_sum_b):
            total[...] = jnp.zeros(total.shape, jnp.float32)

    queries = query[...] * jnp.asarray(HD ** (-0.5), jnp.bfloat16)
    which = pl.program_id(0) ^ spot[1]
    upstream = grad_a[...]
    for k, grad in enumerate((grad_b, grad_c, grad_d)):
        upstream = jnp.where(which == k + 1, grad[...], upstream)
    is_near = pl.program_id(0) // (steps // 2) == spot[0]
    mixed = jnp.where(is_near, mixed_near[...], mixed_away[...])
    log_total = jnp.where(is_near, log_near[...], log_away[...])
    both = upstream.astype(jnp.float32) * mixed
    queries_flat = queries.T
    upstream_flat = upstream.T
    gathered = jnp.zeros(query_grad.shape, jnp.float32)
    blank = jnp.zeros_like(queries)
    for head in range(queries.shape[1] // HD):
        lanes = head_lanes(queries.shape, head)
        own = jnp.where(lanes, queries, blank)
        own_grad = jnp.where(lanes, upstream, blank)
        row_dot = jnp.sum(jnp.where(lanes, both, 0.0), axis=1, keepdims=True)
        total = log_total[:, head : head + 1]
        part = slice(head * HD, (head + 1) * HD)
        result = None
        for key, value, key_sum, value_sum in (
            (key_a, value_a, key_sum_a, value_sum_a),
            (key_b, value_b, key_sum_b, value_sum_b),
        ):
            scores = dot(own, key[...], ROWS)
            probs_grad = dot(own_grad, value[...], ROWS)
            weights = jnp.exp(scores - total)
            score_grad = (weights * (probs_grad - row_dot)).astype(jnp.bfloat16)
            attention = weights.astype(jnp.bfloat16)
            piece = dot(score_grad, key[...], PLAIN)
            result = piece if result is None else result + piece
            key_sum[part, :] += dot(queries_flat[part, :], score_grad, PLAIN)
            value_sum[part, :] += dot(upstream_flat[part, :], attention, PLAIN)
        gathered = jnp.where(lanes, result, gathered)
    query_grad[...] = (gathered * HD ** (-0.5)).astype(jnp.bfloat16)

    @pl.when(pl.program_id(0) == steps - 1)
    def _():
        key_grad_a[...] = key_sum_a[...].T
        value_grad_a[...] = value_sum_a[...].T
        key_grad_b[...] = key_sum_b[...].T.astype(jnp.bfloat16)
        value_grad_b[...] = value_sum_b[...].T.astype(jnp.bfloat16)


def attend_back(spots, queries, grads, near, away, keys, values):
    count, width = queries.shape
    heads = width // HD
    steps = len(grads)
    tile = count // steps
    tokens = keys[0].shape[0]

    def whole(array):
        return pl.BlockSpec(array.shape, lambda i, spot: (0, 0))

    def rows(columns):
        return pl.BlockSpec((tile, columns), lambda i, spot: (i, 0))

    def part(columns):
        return pl.BlockSpec((tile, columns), lambda i, spot: (i % (steps // 2), 0))

    high = jax.ShapeDtypeStruct((tokens, width), jnp.float32)
    low = jax.ShapeDtypeStruct((tokens, width), jnp.bfloat16)
    return pl.pallas_call(
        functools.partial(attend_back_kernel, steps),
        out_shape=(jax.ShapeDtypeStruct((count, width), jnp.bfloat16), high, low, high, low),
        grid_spec=pltpu.PrefetchScalarGridSpec(
            num_scalar_prefetch=1,
            grid=(steps,),
            in_specs=[
                rows(width),
                *[whole(grad) for grad in grads],
                part(width), part(width), part(heads), part(heads),
            ]
            + [whole(array) for array in (*keys, *values)],
            out_specs=(rows(width), whole(high), whole(low), whole(high), whole(low)),
            scratch_shapes=[pltpu.VMEM((width, tokens), jnp.float32) for _ in range(4)],
        ),
        compiler_params=pltpu.CompilerParams(vmem_limit_bytes=48 << 20),
        name="attend_back",
    )(spots, queries, *grads, near[0], away[0], near[1], away[1], *keys, *values)


def project_kernel(count, spots, latent, modulation, bias, *refs):
    pieces = refs[:count]
    normed, query, key, value, weight = refs[count:]
    width = query.shape[1]

    @pl.when(pl.program_id(0) == 0)
    def _():
        for k, piece in enumerate(pieces):
            size = piece.shape[0]
            weight[pl.ds(pl.multiple_of(spots[k] * size, size), size), :] = piece[...]

    rows = modulate_rows(
        latent[...].astype(jnp.float32), modulation[0:1, :], modulation[1:2, :]
    ).astype(jnp.bfloat16)
    normed[...] = rows
    flat = dot(rows, weight[...], PLAIN) + bias[...]
    query[...] = flat[:, :width].astype(jnp.bfloat16)
    key[...] = flat[:, width : 2 * width].astype(jnp.bfloat16)
    value[...] = flat[:, 2 * width :].astype(jnp.bfloat16)


def project(spots, latent, modulation, bias, pieces):
    tokens, features = latent.shape
    columns = bias.shape[1]
    width = columns // 3
    tile = min(256, tokens)

    def still(shape):
        return pl.BlockSpec(shape, lambda i, spots: (0, 0))

    def moving(size):
        return pl.BlockSpec((tile, size), lambda i, spots: (i, 0))

    def low(*shape):
        return jax.ShapeDtypeStruct(shape, jnp.bfloat16)

    return pl.pallas_call(
        functools.partial(project_kernel, len(pieces)),
        out_shape=(
            low(tokens, features),
            low(tokens, width),
            low(tokens, width),
            low(tokens, width),
            low(features, columns),
        ),
        grid_spec=pltpu.PrefetchScalarGridSpec(
            num_scalar_prefetch=1,
            grid=(tokens // tile,),
            in_specs=[moving(features), still(modulation.shape), still(bias.shape)]
            + [still(piece.shape) for piece in pieces],
            out_specs=(
                moving(features),
                moving(width),
                moving(width),
                moving(width),
                still((features, columns)),
            ),
        ),
        compiler_params=pltpu.CompilerParams(vmem_limit_bytes=48 << 20),
        name="project",
    )(spots, latent, modulation, bias, *pieces)


def project_back_kernel(
    spots, query, key_a, key_b, value_a, value_b, latent, weight,
    grad_a, grad_b, grad_c, grad_d, joined, sums, token_sums,
):
    @pl.when(pl.program_id(0) == 0)
    def _():
        sums[...] = jnp.zeros(sums.shape, jnp.float32)
        token_sums[...] = jnp.zeros(token_sums.shape, jnp.float32)

    flat = jnp.concatenate(
        [
            query[...],
            (key_a[...] + key_b[...].astype(jnp.float32)).astype(jnp.bfloat16),
            (value_a[...] + value_b[...].astype(jnp.float32)).astype(jnp.bfloat16),
        ],
        axis=1,
    )
    joined[...] = flat
    sums[...] += jnp.sum(flat.astype(jnp.float32), axis=0, keepdims=True)
    result = dot(flat, weight[...], ROWS)
    normed = normalise(latent[...].astype(jnp.float32))[0]
    token_sums[0:1, :] += row_sum(result)
    token_sums[1:2, :] += row_sum(result * normed)
    result = result.astype(jnp.bfloat16)
    for k, grad in enumerate((grad_a, grad_b, grad_c, grad_d)):

        @pl.when(pl.program_id(0) == k)
        def _(grad=grad):
            grad[...] = result


def project_back(held_back, spots, query, key_a, key_b, value_a, value_b, latent, weight):
    tokens, width = query.shape
    features, columns = weight.shape
    tile = tokens // 4

    def moving(size):
        return pl.BlockSpec((tile, size), lambda i, spots: (spots[i], 0))

    def still(shape):
        return pl.BlockSpec(shape, lambda i, spots: (0, 0))

    piece = jax.ShapeDtypeStruct((tile, features), jnp.bfloat16)
    return pl.pallas_call(
        after(len(held_back), project_back_kernel),
        out_shape=(
            piece,
            piece,
            piece,
            piece,
            jax.ShapeDtypeStruct((tokens, columns), jnp.bfloat16),
            jax.ShapeDtypeStruct((1, columns), jnp.float32),
            jax.ShapeDtypeStruct((8, features), jnp.float32),
        ),
        grid_spec=pltpu.PrefetchScalarGridSpec(
            num_scalar_prefetch=1,
            grid=(4,),
            in_specs=held(held_back)
            + [moving(width)] * 5 + [moving(features), still(weight.shape)],
            out_specs=(still(piece.shape),) * 4
            + (moving(columns), still((1, columns)), still((8, features))),
        ),
        compiler_params=pltpu.CompilerParams(vmem_limit_bytes=48 << 20),
        name="project_back",
    )(spots, *held_back, query, key_a, key_b, value_a, value_b, latent, weight)


def row_sum(values):
    return jnp.sum(values, axis=0, keepdims=True)


def middle_back_kernel(
    spots, latent, cotangent, branch_one, grad_here, grad_there, modulation, merge,
    middle, middle_grad, branch_one_grad, piece_a, piece_b, piece_c, piece_d, sums,
):
    branch = branch_one[...]
    upstream = cotangent[...].astype(jnp.float32)
    centre = latent[...].astype(jnp.float32) + modulation[2:3, :] * branch
    middle[...] = centre
    normed, scale = normalise(centre)
    grad = grad_here[...].astype(jnp.float32) + grad_there[...].astype(jnp.float32)
    total = upstream + normalise_back(grad * (1.0 + modulation[4:5, :]), normed, scale)
    middle_grad[...] = total
    branch_grad = (modulation[2:3, :] * total).astype(jnp.bfloat16)
    branch_one_grad[...] = branch_grad
    mixed = dot(branch_grad, merge[...], PLAIN).astype(jnp.bfloat16)
    width = piece_a.shape[1]
    for k, piece in enumerate((piece_a, piece_b, piece_c, piece_d)):
        piece[...] = mixed[:, k * width : (k + 1) * width]
    scaled = (modulation[5:6, :] * upstream).astype(jnp.bfloat16).astype(jnp.float32)
    sums[0:1, :] = row_sum(total * branch)
    sums[1:2, :] = row_sum(grad)
    sums[2:3, :] = row_sum(grad * normed)
    sums[3:4, :] = row_sum(branch_grad.astype(jnp.float32))
    sums[4:5, :] = row_sum(scaled)
    sums[5:8, :] = jnp.zeros((3, sums.shape[1]), jnp.float32)


def middle_back(held_back, spots, latent, cotangent, branch_one, here, there, modulation, far, width):
    count, features = here.shape

    def still(shape):
        return pl.BlockSpec(shape, lambda i, spots: (0, 0))

    def picked(place_at):
        return pl.BlockSpec((count, features), lambda i, spots: (spots[place_at], 0))

    def low(*shape):
        return jax.ShapeDtypeStruct(shape, jnp.bfloat16)

    def high(*shape):
        return jax.ShapeDtypeStruct(shape, jnp.float32)

    shapes = (
        high(count, features),
        high(count, features),
        low(count, features),
        low(count, width),
        low(count, width),
        low(count, width),
        low(count, width),
        high(8, features),
    )
    return pl.pallas_call(
        after(len(held_back), middle_back_kernel),
        out_shape=shapes,
        grid_spec=pltpu.PrefetchScalarGridSpec(
            num_scalar_prefetch=1,
            grid=(1,),
            in_specs=held(held_back)
            + [
                picked(0),
                picked(0),
                picked(1),
                still(here.shape),
                still(there.shape),
                still(modulation.shape),
                still((features, features)),
            ],
            out_specs=tuple(still(shape.shape) for shape in shapes),
        ),
        compiler_params=pltpu.CompilerParams(vmem_limit_bytes=48 << 20),
        name="middle_back",
    )(spots, *held_back, latent, cotangent, branch_one, here, there, modulation, far)


def latent_back_kernel(spots, latent, middle_grad, modulation, part_a, part_b, part_c, result):
    normed, scale = normalise(latent[...].astype(jnp.float32))
    grad = (
        part_a[...].astype(jnp.float32)
        + part_b[...].astype(jnp.float32)
        + part_c[...].astype(jnp.float32)
    )
    total = middle_grad[...] + normalise_back(grad * (1.0 + modulation[1:2, :]), normed, scale)
    result[...] = total.astype(jnp.bfloat16)


def latent_back(spots, latent, middle_grad, modulation, parts):
    count, features = middle_grad.shape

    def still(shape):
        return pl.BlockSpec(shape, lambda i, spots: (0, 0))

    square = still((count, features))
    return pl.pallas_call(
        latent_back_kernel,
        out_shape=jax.ShapeDtypeStruct((count, features), jnp.bfloat16),
        grid_spec=pltpu.PrefetchScalarGridSpec(
            num_scalar_prefetch=1,
            grid=(1,),
            in_specs=[
                pl.BlockSpec((count, features), lambda i, spots: (spots[0], 0)),
                square,
                still(modulation.shape),
                square,
                square,
                square,
            ],
            out_specs=square,
        ),
        compiler_params=pltpu.CompilerParams(vmem_limit_bytes=48 << 20),
        name="latent_back",
    )(spots, latent, middle_grad, modulation, *parts)


def modulate_rows(values, offset, scaling):
    return normalise(values)[0] * (1.0 + scaling) + offset


def smooth_gate_both(values):
    cubic = math.sqrt(2.0 / math.pi) * (values + 0.044715 * values * values * values)
    slope = math.sqrt(2.0 / math.pi) * (1.0 + 3.0 * 0.044715 * values * values)
    bend = jnp.tanh(cubic)
    lifted = 0.5 * (1.0 + bend)
    return values * lifted, lifted + 0.5 * values * (1.0 - bend * bend) * slope


def forward_back_kernel(
    steps,
    spot,
    piece_a, piece_b, piece_c, piece_d,
    latent, cotangent, modulation, merge, merge_bias,
    expand_near, expand_far, reduce_near, reduce_far, bias,
    branch_one, normed_two, branch_two_grad, activated, hidden_grad, bias_grad,
    branch_two_here, branch_two_there, grad_here, grad_there,
    forward_sum, backward_sum,
):
    step = pl.program_id(0)

    @pl.when(step == 0)
    def _():
        mixture = jnp.concatenate(
            [piece_a[...], piece_b[...], piece_c[...], piece_d[...]], axis=1
        )
        branch = dot(mixture, merge[...], ROWS) + merge_bias[...].astype(jnp.float32)
        branch_one[...] = branch
        middle = latent[...].astype(jnp.float32) + modulation[2:3, :] * branch
        normed_two[...] = modulate_rows(
            middle, modulation[3:4, :], modulation[4:5, :]
        ).astype(jnp.bfloat16)
        branch_two_grad[...] = (
            modulation[5:6, :] * cotangent[...].astype(jnp.float32)
        ).astype(jnp.bfloat16)
        forward_sum[...] = jnp.zeros(forward_sum.shape, jnp.float32)
        backward_sum[...] = jnp.zeros(backward_sum.shape, jnp.float32)

    def block(expand, reduce):
        hidden = dot(normed_two[...], expand[...], PLAIN) + bias[...].astype(jnp.float32)
        value, slope = smooth_gate_both(hidden)
        value = value.astype(jnp.bfloat16)
        activated[...] = value
        grad = dot(branch_two_grad[...], reduce[...], PLAIN) * slope
        grad = grad.astype(jnp.bfloat16)
        hidden_grad[...] = grad
        bias_grad[...] = jnp.sum(grad.astype(jnp.float32), axis=0, keepdims=True)
        backward_sum[...] += dot(grad, expand[...], ROWS)
        forward_sum[...] += dot(value, reduce[...], ROWS)

    @pl.when(step < steps // 2)
    def _():
        block(expand_near, reduce_near)

    @pl.when(step >= steps // 2)
    def _():
        block(expand_far, reduce_far)

    @pl.when(step == steps - 1)
    def _():
        count = grad_here.shape[0]
        here = pl.ds(pl.multiple_of(spot[1] * count, count), count)
        there = pl.ds(pl.multiple_of((1 - spot[1]) * count, count), count)
        branch_two_here[...] = forward_sum[here, :].astype(jnp.bfloat16)
        branch_two_there[...] = forward_sum[there, :].astype(jnp.bfloat16)
        grad_here[...] = backward_sum[here, :].astype(jnp.bfloat16)
        grad_there[...] = backward_sum[there, :].astype(jnp.bfloat16)


def forward_back(spots, pieces, latent, cotangent, modulation, near, far, merge_bias, bias):
    rows, width = pieces[0].shape
    features = latent.shape[1]
    hidden = bias.shape[1] // 2
    tile = min(512, hidden)
    per = hidden // tile
    steps = 2 * per
    ahead = features // tile

    def still(array):
        return pl.BlockSpec(array.shape, lambda j, spot: (0, 0))

    def picked():
        return pl.BlockSpec((rows, features), lambda j, spot: (spot[0], 0))

    def column(first, lag):
        def place_at(j, spot):
            return (0, first + jnp.clip(j - lag, 0, per - 1))

        return pl.BlockSpec((features, tile), place_at)

    moving = pl.BlockSpec((rows, tile), lambda j, spot: (0, j))
    row_tile = pl.BlockSpec((1, tile), lambda j, spot: (0, j))
    square = pl.BlockSpec((rows, features), lambda j, spot: (0, 0))
    piece = pl.BlockSpec((rows // 2, features), lambda j, spot: (0, 0))
    low = jax.ShapeDtypeStruct((rows, features), jnp.bfloat16)
    high = jax.ShapeDtypeStruct((rows, features), jnp.float32)
    lower = jax.ShapeDtypeStruct((rows // 2, features), jnp.bfloat16)
    return pl.pallas_call(
        functools.partial(forward_back_kernel, steps),
        out_shape=(
            high,
            low,
            low,
            jax.ShapeDtypeStruct((rows, 2 * hidden), jnp.bfloat16),
            jax.ShapeDtypeStruct((rows, 2 * hidden), jnp.bfloat16),
            jax.ShapeDtypeStruct((1, 2 * hidden), jnp.float32),
            lower,
            lower,
            lower,
            lower,
        ),
        grid_spec=pltpu.PrefetchScalarGridSpec(
            num_scalar_prefetch=1,
            grid=(steps,),
            in_specs=[still(piece) for piece in pieces]
            + [
                picked(),
                picked(),
                still(modulation),
                pl.BlockSpec((features, features), lambda j, spot: (0, 0)),
                still(merge_bias),
                column(0, 0),
                column(ahead, per),
                column(per, 0),
                column(ahead + per, per),
                row_tile,
            ],
            out_specs=(square, square, square, moving, moving, row_tile, piece, piece, piece, piece),
            scratch_shapes=[
                pltpu.VMEM((rows, features), jnp.float32),
                pltpu.VMEM((rows, features), jnp.float32),
            ],
        ),
        compiler_params=pltpu.CompilerParams(vmem_limit_bytes=58 << 20),
        name="forward_back",
    )(spots, *pieces, latent, cotangent, modulation, far, merge_bias, near, far, near, far, bias)


def weight_grad_kernel(
    per, waited, first_left, first_right, second_left, second_right, result, turned, turned_second
):
    step = pl.program_id(0)

    @pl.when(step == 0)
    def _():
        turned[...] = first_left[...].T

    @pl.when(step == per)
    def _():
        turned_second[...] = second_left[...].T

    @pl.when(step < per)
    def _():
        result[...] = dot(turned[...], first_right[...], PLAIN).astype(jnp.bfloat16)

    @pl.when(step >= per)
    def _():
        result[...] = dot(turned_second[...], second_right[...], PLAIN).astype(jnp.bfloat16)


def weight_grads(held_back, first_left, first_right, second_left, second_right, tile):
    features = first_left.shape[1]
    per = first_right.shape[1] // tile
    more = second_right.shape[1] // tile

    def still(array):
        return pl.BlockSpec(array.shape, lambda j, spot: (0, 0))

    return pl.pallas_call(
        after(len(held_back), functools.partial(weight_grad_kernel, per)),
        out_shape=jax.ShapeDtypeStruct((features, (per + more) * tile), jnp.bfloat16),
        grid_spec=pltpu.PrefetchScalarGridSpec(
        num_scalar_prefetch=1,
        grid=(per + more,),
        in_specs=held(held_back)
        + [
            still(first_left),
            pl.BlockSpec((first_right.shape[0], tile), lambda j, spot: (0, jnp.minimum(j, per - 1))),
            still(second_left),
            pl.BlockSpec((second_right.shape[0], tile), lambda j, spot: (0, jnp.maximum(j - per, 0))),
        ],
        out_specs=pl.BlockSpec((features, tile), lambda j, spot: (0, j)),
        scratch_shapes=[
            pltpu.VMEM((features, first_left.shape[0]), jnp.bfloat16),
            pltpu.VMEM((features, second_left.shape[0]), jnp.bfloat16),
        ],
        ),
        compiler_params=pltpu.CompilerParams(vmem_limit_bytes=48 << 20),
        name="weight_grads",
    )(jnp.zeros((1,), jnp.int32), *held_back, first_left, first_right, second_left, second_right)


def body(
    sizes,
    latents,
    condition,
    modulation_weight,
    modulation_bias,
    heads_weight,
    heads_bias,
    merge_weight,
    merge_bias,
    expand_weight,
    expand_bias,
    reduce_weight,
    reduce_bias,
    cotangent,
):
    n_shard, n_ctx, n_tp = sizes
    if n_tp != 4 or latents.shape[0] != 1:
        raise ValueError("unsupported split")
    wide = jnp.float32
    narrow = jnp.bfloat16
    owners = ("shard", "ctx")
    row_block = lax.axis_index("shard") * n_ctx + lax.axis_index("ctx")
    tp_index = lax.axis_index("tp")
    pair = tp_index // 2
    side = tp_index % 2
    feature_rows = modulation_weight.shape[0]
    width = modulation_weight.shape[2]
    hidden_width = expand_weight.shape[1]
    latent = latents[0]
    tokens, features = latent.shape
    group = tokens // 2
    count = tokens // n_tp

    def once(values, token):
        return values + token.astype(values.dtype)

    conditions = gather_small(condition[0], "shard", n_shard)
    started = blank_after(conditions)
    heads_flat = once(heads_weight.reshape(feature_rows, 3 * width), started)
    if n_shard > 8 or n_ctx != 2:
        heads_rows = None
    else:
        heads_rows = swapped(heads_flat, "shard", n_shard)
    far = swap(
        jnp.concatenate([merge_weight, expand_weight, reduce_weight], axis=1), "tp", n_tp, 2
    )
    merge_started = once(merge_weight, started)
    merge_near = swap(merge_started, "tp", n_tp, 1)
    merge_last = swap(merge_started, "tp", n_tp, 3)
    near_full = lax.all_gather(
        jnp.concatenate([expand_weight, reduce_weight], axis=1), owners, axis=0, tiled=True
    )
    silu_rows = jax.nn.silu(
        lax.dynamic_slice_in_dim(conditions, row_block * feature_rows, feature_rows, 1).astype(wide)
    ).astype(narrow)
    partial = product("ld,dkf->lkf", silu_rows, modulation_weight)
    local_modulation = scatter_small(partial, "shard", n_shard)
    local_modulation = add_all(local_modulation, "ctx", n_ctx) + modulation_bias.astype(wide)
    bias_away = swap(expand_bias, "tp", n_tp, 2)
    for early in [bias_away] + (heads_rows or [])[1:]:
        local_modulation = local_modulation + blank_after(early)
    modulation = gather_small(local_modulation, "tp", n_tp)
    modulation = jnp.swapaxes(modulation, 0, 1).reshape(6, features)
    offset_one, scaling_one, gate_one, offset_two, scaling_two, gate_two = (
        modulation[k][None] for k in range(6)
    )
    issued = blank_after(local_modulation)
    far_rows = jnp.concatenate(
        [merge_weight, merge_near, far[:, :width], merge_last, far[:, width:]], axis=1
    )
    far_full = lax.all_gather(
        far_rows + issued.astype(narrow), owners, axis=0, tiled=True
    )
    if heads_rows is None:
        heads_pieces = [lax.all_gather(heads_flat, owners, axis=0, tiled=True)]
        spots = jnp.zeros((1,), jnp.int32)
    else:
        shard = lax.axis_index("shard")
        ctx = lax.axis_index("ctx")
        heads_other = [swap(once(rows, issued), "ctx", n_ctx, 1) for rows in heads_rows]
        heads_pieces = heads_rows + heads_other
        places = [(shard ^ k) * n_ctx for k in range(n_shard)]
        spots = jnp.stack([p + ctx for p in places] + [p + 1 - ctx for p in places])
    expand_biases = jnp.concatenate([expand_bias, bias_away])[None]

    bias_rows = heads_bias.astype(wide)
    project_bias = jnp.concatenate([bias_rows[0], jnp.zeros_like(bias_rows[0]), bias_rows[1]])
    normed_one, queries, keys_here, values_here, heads_full = project(
        spots, latent, modulation, project_bias[None], heads_pieces
    )
    keys = (keys_here, swap(keys_here, "ctx", n_ctx, 1))
    values = (values_here, swap(values_here, "ctx", n_ctx, 1))

    mixed_away, *kept_away = attend(1 - pair, group, queries, keys, values)
    mixed_near, *kept_near = attend(pair, group, queries, keys, values)
    across = swap(mixed_away, "tp", n_tp, 2)
    pieces = [mixed_near, swap(mixed_near, "tp", n_tp, 1), across, swap(across, "tp", n_tp, 1)]
    (
        branch_one,
        normed_two,
        branch_two_grad,
        activated,
        hidden_grad,
        hidden_bias_grad,
        branch_two_here,
        branch_two_there,
        grad_here,
        grad_there,
    ) = forward_back(
        jnp.stack([pair, side]),
        pieces,
        latent,
        cotangent[0],
        modulation,
        near_full,
        far_full,
        merge_bias[None],
        expand_biases,
    )
    arrived = swap(grad_there, "tp", n_tp, 1)
    hidden_grads = weight_grads(
        [], branch_two_grad, activated, normed_two, hidden_grad, min(512, hidden_width)
    )
    middle, middle_grad, branch_one_grad, *mixture_grads, second_sums = middle_back(
        [hidden_grads],
        jnp.stack([tp_index, side]),
        latent,
        cotangent[0],
        branch_one,
        grad_here,
        arrived,
        modulation,
        far_full,
        width,
    )
    received = [
        swap(mixture_grads[k], "tp", n_tp, k) if k else mixture_grads[0] for k in range(n_tp)
    ]
    scattered = lax.psum_scatter(
        hidden_grads,
        owners,
        scatter_dimension=0,
        tiled=True,
    )

    arrived_two = swap(branch_two_there, "tp", n_tp, 1)
    branch_two = (
        branch_two_here.astype(wide)
        + arrived_two.astype(wide)
        + reduce_bias.astype(wide)
    )
    own_output = (middle + gate_two * branch_two).astype(narrow)
    output_pieces = spread(own_output)
    output = assembled(output_pieces)
    gate_two_grad = jnp.sum(
        block_of(cotangent[0], tp_index, count).astype(wide) * branch_two, axis=0, keepdims=True
    )

    query_grad, key_grad_a, key_grad_b, value_grad_a, value_grad_b = attend_back(
        jnp.stack([pair, tp_index]), queries, received, kept_near, kept_away, keys, values
    )
    here, by_one, by_two, by_three, projected_grad, projected_sums, first_sums = project_back(
        output_pieces[1:3],
        jnp.stack([tp_index ^ k for k in range(n_tp)]),
        query_grad,
        key_grad_a,
        swap(key_grad_b, "ctx", n_ctx, 1),
        value_grad_a,
        swap(value_grad_b, "ctx", n_ctx, 1),
        latent,
        heads_full,
    )
    heads_bias_grad = jnp.concatenate(
        [projected_sums[0, :width], projected_sums[0, 2 * width :]]
    )
    beside = swap(by_three, "tp", n_tp, 1)
    from_far = [
        swap((by_two.astype(wide) + beside.astype(wide)).astype(narrow), "tp", n_tp, 2)
    ]
    near_sum = swap(once(by_one, blank_after(beside)), "tp", n_tp, 1)
    own_mixture = jnp.concatenate([block_of(piece, side, count) for piece in pieces], axis=1)
    scattered_more = lax.psum_scatter(
        weight_grads(
            [scattered, beside], normed_one, projected_grad, branch_one_grad, own_mixture, width),
        owners,
        scatter_dimension=0,
        tiled=True,
    )
    heads_weight_grad = scattered_more[:, : 3 * width].astype(wide)
    merge_pieces = scattered_more[:, 3 * width :]
    reduce_near, reduce_far, expand_near, expand_far = (
        scattered[:, k * hidden_width : (k + 1) * hidden_width] for k in range(4)
    )
    far_pair = jnp.concatenate([reduce_far, expand_far], axis=1)
    both = swap(far_pair, "tp", n_tp, 2).astype(wide)
    reduce_weight_grad = reduce_near.astype(wide) + both[:, :hidden_width]
    expand_weight_grad = expand_near.astype(wide) + both[:, hidden_width:]
    merge_weight_grad = merge_pieces[:, :width].astype(wide)
    for k in range(1, n_tp):
        merge_weight_grad = merge_weight_grad + swap(
            merge_pieces[:, k * width : (k + 1) * width], "tp", n_tp, k
        ).astype(wide)
    expand_bias_grad = hidden_bias_grad[0, :hidden_width] + swap(
        hidden_bias_grad[0, hidden_width:], "tp", n_tp, 2
    )
    sums = jnp.concatenate([second_sums[:3], gate_two_grad, second_sums[3:5]], axis=0)
    first_sums = first_sums[:2]

    own_grad = latent_back(
        tp_index[None],
        latent,
        middle_grad,
        modulation,
        (here, near_sum, *from_far),
    )
    latent_pieces = spread(own_grad)
    vectors = jnp.concatenate([first_sums, sums], axis=0)
    vectors = vectors + blank_after(latent_pieces[1]) + blank_after(latent_pieces[2])
    vectors = vectors + blank_after(both)
    vectors = add_all(vectors, "tp", n_tp)
    local_grad = lax.dynamic_slice_in_dim(vectors[:6], tp_index * width, width, 1)
    common = jnp.concatenate(
        [
            local_grad.reshape(-1),
            vectors[6],
            vectors[7],
            expand_bias_grad,
            heads_bias_grad,
        ]
    )
    common = add_all(common, "ctx", n_ctx)
    local_grad = common[: 6 * width].reshape(6, width)
    biases = add_all(common[6 * width :], "shard", n_shard)
    modulation_grad = gather_small(local_grad, "shard", n_shard)
    modulation_bias_grad = jnp.sum(modulation_grad, axis=0)
    modulation_weight_grad = jnp.einsum(
        "ld,lkf->dkf", silu_rows.astype(wide), modulation_grad, precision=lax.Precision.HIGHEST
    )
    latents_grad = assembled(latent_pieces).astype(wide)
    cuts = [features, features, hidden_width, 2 * width]
    edges = [sum(cuts[:k]) for k in range(len(cuts) + 1)]
    merge_bias_grad, reduce_bias_grad, expand_bias_grad, heads_bias_grad = (
        biases[edges[k] : edges[k + 1]] for k in range(4)
    )
    return (
        output[None],
        latents_grad[None],
        modulation_weight_grad,
        modulation_bias_grad,
        heads_weight_grad.reshape(feature_rows, 3, width),
        heads_bias_grad.reshape(2, width),
        merge_weight_grad,
        merge_bias_grad,
        expand_weight_grad,
        expand_bias_grad,
        reduce_weight_grad,
        reduce_bias_grad,
    )


def solution(mesh):
    sizes = tuple(mesh.shape[name] for name in ("shard", "ctx", "tp"))
    return jax.shard_map(
        functools.partial(body, sizes),
        mesh=mesh,
        in_specs=(
            P("shard", "ctx", None),
            P("shard", None),
            P(("shard", "ctx"), None, "tp"),
            P(None, "tp"),
            P(("shard", "ctx"), None, "tp"),
            P(None, "tp"),
            P(("shard", "ctx"), "tp"),
            P(),
            P(("shard", "ctx"), "tp"),
            P("tp"),
            P(("shard", "ctx"), "tp"),
            P(),
            P("shard", "ctx", None),
        ),
        out_specs=(
            P("shard", "ctx", None),
            P("shard", "ctx", None),
            P(("shard", "ctx"), None, "tp"),
            P(None, "tp"),
            P(("shard", "ctx"), None, "tp"),
            P(None, "tp"),
            P(("shard", "ctx"), "tp"),
            P(),
            P(("shard", "ctx"), "tp"),
            P("tp"),
            P(("shard", "ctx"), "tp"),
            P(),
        ),
        check_vma=False,
    )
```

```python
import functools
import math

import jax
import jax.numpy as jnp
from jax import lax
from jax.experimental import pallas as pl
from jax.experimental.pallas import tpu as pltpu
from jax.sharding import PartitionSpec as P

HD = 64


def swap(values, axis, size, distance):
    return lax.ppermute(values, axis, [(i, i ^ distance) for i in range(size)])


def swapped(values, axis, size):
    return [values] + [swap(values, axis, size, k) for k in range(1, size)]


def add_all(values, axis, size):
    step = 1
    while step < size:
        values = values + swap(values, axis, size, step)
        step *= 2
    return values


def gather_small(values, axis, size):
    if size > 8:
        return lax.all_gather(values, axis)
    pieces = swapped(values, axis, size)
    here = lax.axis_index(axis)
    rows = []
    for j in range(size):
        row = pieces[0]
        for k in range(1, size):
            row = jnp.where((here ^ j) == k, pieces[k], row)
        rows.append(row)
    return jnp.stack(rows)


def scatter_small(values, axis, size):
    if size > 8:
        return lax.psum_scatter(values, axis)
    here = lax.axis_index(axis)

    def piece(k):
        return lax.dynamic_index_in_dim(values, here ^ k, 0, keepdims=False)

    total = piece(0)
    for k in range(1, size):
        total = total + swap(piece(k), axis, size, k)
    return total


def zero_after(values):
    corner = lax.slice(values, (0,) * values.ndim, (1,) * values.ndim).reshape(())
    return (corner.astype(jnp.float32) * 0.0).astype(jnp.int32)


def blank_after(values):
    corner = lax.slice(values, (0,) * values.ndim, (1,) * values.ndim).reshape(())
    return corner.astype(jnp.float32) * 0.0


def block_of(values, index, count):
    return lax.dynamic_slice_in_dim(values, index * count, count, 0)


def place(whole, piece, index):
    return lax.dynamic_update_slice_in_dim(whole, piece, index * piece.shape[0], 0)


def spread(values):
    across = swap(values, "tp", 4, 2)
    return values, swap(values, "tp", 4, 1), across, swap(across, "tp", 4, 1)


def assembled(pieces, blank=0.0):
    here = lax.axis_index("tp")
    count = pieces[0].shape[0]
    whole = jnp.zeros((4 * count,) + pieces[0].shape[1:], pieces[0].dtype)
    whole = whole + jnp.asarray(blank).astype(whole.dtype)
    for k, piece in enumerate(pieces):
        whole = place(whole, piece, here ^ k)
    return whole


def normalise(values):
    centre = values - jnp.mean(values, axis=-1, keepdims=True)
    variance = jnp.mean(centre * centre, axis=-1, keepdims=True)
    scale = lax.rsqrt(variance + 1e-06)
    return centre * scale, scale


def normalise_back(grad, normed, scale):
    inner = grad - jnp.mean(grad, axis=-1, keepdims=True)
    return scale * (inner - normed * jnp.mean(grad * normed, axis=-1, keepdims=True))


def smooth_gate(values):
    return jax.nn.gelu(values, approximate=True)


def product(text, left, right):
    return jnp.einsum(text, left, right, preferred_element_type=jnp.float32)


def after(count, kernel):
    def run(spot, *refs):
        kernel(spot, *refs[count:])

    return run


def held(arrays):
    return [pl.BlockSpec(memory_space=pl.ANY) for _ in arrays]


def head_lanes(shape, head):
    lane = lax.broadcasted_iota(jnp.int32, shape, 1)
    return (lane >= head * HD) & (lane < (head + 1) * HD)


def dot(left, right, dims):
    return lax.dot_general(left, right, (dims, ((), ())), preferred_element_type=jnp.float32)


ROWS = ((1,), (1,))
PLAIN = ((1,), (0,))


def attend_kernel(spot, query, key_a, key_b, value_a, value_b, mixed, mixed_wide, log_total):
    queries = query[...] * jnp.asarray(HD ** (-0.5), jnp.bfloat16)
    gathered = jnp.zeros(mixed_wide.shape, jnp.float32)
    for head in range(queries.shape[1] // HD):
        lanes = head_lanes(queries.shape, head)
        own = jnp.where(lanes, queries, jnp.zeros_like(queries))
        score_a = dot(own, key_a[...], ROWS)
        score_b = dot(own, key_b[...], ROWS)
        top = jnp.maximum(
            jnp.max(score_a, axis=1, keepdims=True), jnp.max(score_b, axis=1, keepdims=True)
        )
        exp_a = jnp.exp(score_a - top)
        exp_b = jnp.exp(score_b - top)
        summed = jnp.sum(exp_a, axis=1, keepdims=True) + jnp.sum(exp_b, axis=1, keepdims=True)
        blend = dot(exp_a.astype(jnp.bfloat16), value_a[...], PLAIN)
        blend = blend + dot(exp_b.astype(jnp.bfloat16), value_b[...], PLAIN)
        gathered = jnp.where(lanes, blend / summed, gathered)
        log_total[:, head : head + 1] = top + jnp.log(summed)
    mixed[...] = gathered.astype(jnp.bfloat16)
    mixed_wide[...] = gathered


def attend(block, count, queries, keys, values):
    width = queries.shape[1]
    heads = width // HD
    tile = min(512, count)
    steps = count // tile

    def whole(array):
        return pl.BlockSpec(array.shape, lambda i, spot: (0, 0))

    def rows(columns):
        return pl.BlockSpec((tile, columns), lambda i, spot: (i, 0))

    return pl.pallas_call(
        attend_kernel,
        out_shape=(
            jax.ShapeDtypeStruct((count, width), jnp.bfloat16),
            jax.ShapeDtypeStruct((count, width), jnp.float32),
            jax.ShapeDtypeStruct((count, heads), jnp.float32),
        ),
        grid_spec=pltpu.PrefetchScalarGridSpec(
            num_scalar_prefetch=1,
            grid=(steps,),
            in_specs=[pl.BlockSpec((tile, width), lambda i, spot: (spot[0] * steps + i, 0))]
            + [whole(array) for array in (*keys, *values)],
            out_specs=(rows(width), rows(width), rows(heads)),
        ),
        compiler_params=pltpu.CompilerParams(vmem_limit_bytes=48 << 20),
        name="attend",
    )(block[None], queries, *keys, *values)


def attend_back_kernel(
    steps,
    spot, query, grad_a, grad_b, grad_c, grad_d, mixed_near, mixed_away, log_near, log_away,
    key_a, key_b, value_a, value_b,
    query_grad, key_grad_a, key_grad_b, value_grad_a, value_grad_b,
    key_sum_a, key_sum_b, value_sum_a, value_sum_b,
):
    @pl.when(pl.program_id(0) == 0)
    def _():
        for total in (key_sum_a, key_sum_b, value_sum_a, value_sum_b):
            total[...] = jnp.zeros(total.shape, jnp.float32)

    queries = query[...] * jnp.asarray(HD ** (-0.5), jnp.bfloat16)
    which = pl.program_id(0) ^ spot[1]
    upstream = grad_a[...]
    for k, grad in enumerate((grad_b, grad_c, grad_d)):
        upstream = jnp.where(which == k + 1, grad[...], upstream)
    is_near = pl.program_id(0) // (steps // 2) == spot[0]
    mixed = jnp.where(is_near, mixed_near[...], mixed_away[...])
    log_total = jnp.where(is_near, log_near[...], log_away[...])
    both = upstream.astype(jnp.float32) * mixed
    queries_flat = queries.T
    upstream_flat = upstream.T
    gathered = jnp.zeros(query_grad.shape, jnp.float32)
    blank = jnp.zeros_like(queries)
    for head in range(queries.shape[1] // HD):
        lanes = head_lanes(queries.shape, head)
        own = jnp.where(lanes, queries, blank)
        own_grad = jnp.where(lanes, upstream, blank)
        row_dot = jnp.sum(jnp.where(lanes, both, 0.0), axis=1, keepdims=True)
        total = log_total[:, head : head + 1]
        part = slice(head * HD, (head + 1) * HD)
        result = None
        for key, value, key_sum, value_sum in (
            (key_a, value_a, key_sum_a, value_sum_a),
            (key_b, value_b, key_sum_b, value_sum_b),
        ):
            scores = dot(own, key[...], ROWS)
            probs_grad = dot(own_grad, value[...], ROWS)
            weights = jnp.exp(scores - total)
            score_grad = (weights * (probs_grad - row_dot)).astype(jnp.bfloat16)
            attention = weights.astype(jnp.bfloat16)
            piece = dot(score_grad, key[...], PLAIN)
            result = piece if result is None else result + piece
            key_sum[part, :] += dot(queries_flat[part, :], score_grad, PLAIN)
            value_sum[part, :] += dot(upstream_flat[part, :], attention, PLAIN)
        gathered = jnp.where(lanes, result, gathered)
    query_grad[...] = (gathered * HD ** (-0.5)).astype(jnp.bfloat16)

    @pl.when(pl.program_id(0) == steps - 1)
    def _():
        key_grad_a[...] = key_sum_a[...].T
        value_grad_a[...] = value_sum_a[...].T
        key_grad_b[...] = key_sum_b[...].T.astype(jnp.bfloat16)
        value_grad_b[...] = value_sum_b[...].T.astype(jnp.bfloat16)


def attend_back(spots, queries, grads, near, away, keys, values):
    count, width = queries.shape
    heads = width // HD
    steps = len(grads)
    tile = count // steps
    tokens = keys[0].shape[0]

    def whole(array):
        return pl.BlockSpec(array.shape, lambda i, spot: (0, 0))

    def rows(columns):
        return pl.BlockSpec((tile, columns), lambda i, spot: (i, 0))

    def part(columns):
        return pl.BlockSpec((tile, columns), lambda i, spot: (i % (steps // 2), 0))

    high = jax.ShapeDtypeStruct((tokens, width), jnp.float32)
    low = jax.ShapeDtypeStruct((tokens, width), jnp.bfloat16)
    return pl.pallas_call(
        functools.partial(attend_back_kernel, steps),
        out_shape=(jax.ShapeDtypeStruct((count, width), jnp.bfloat16), high, low, high, low),
        grid_spec=pltpu.PrefetchScalarGridSpec(
            num_scalar_prefetch=1,
            grid=(steps,),
            in_specs=[
                rows(width),
                *[whole(grad) for grad in grads],
                part(width), part(width), part(heads), part(heads),
            ]
            + [whole(array) for array in (*keys, *values)],
            out_specs=(rows(width), whole(high), whole(low), whole(high), whole(low)),
            scratch_shapes=[pltpu.VMEM((width, tokens), jnp.float32) for _ in range(4)],
        ),
        compiler_params=pltpu.CompilerParams(vmem_limit_bytes=48 << 20),
        name="attend_back",
    )(spots, queries, *grads, near[0], away[0], near[1], away[1], *keys, *values)


def project_kernel(count, spots, latent, modulation, bias, *refs):
    pieces = refs[:count]
    normed, query, key, value, weight = refs[count:]
    width = query.shape[1]

    @pl.when(pl.program_id(0) == 0)
    def _():
        for k, piece in enumerate(pieces):
            size = piece.shape[0]
            weight[pl.ds(pl.multiple_of(spots[k] * size, size), size), :] = piece[...]

    rows = modulate_rows(
        latent[...].astype(jnp.float32), modulation[0:1, :], modulation[1:2, :]
    ).astype(jnp.bfloat16)
    normed[...] = rows
    flat = dot(rows, weight[...], PLAIN) + bias[...]
    query[...] = flat[:, :width].astype(jnp.bfloat16)
    key[...] = flat[:, width : 2 * width].astype(jnp.bfloat16)
    value[...] = flat[:, 2 * width :].astype(jnp.bfloat16)


def project(spots, latent, modulation, bias, pieces):
    tokens, features = latent.shape
    columns = bias.shape[1]
    width = columns // 3
    tile = min(256, tokens)

    def still(shape):
        return pl.BlockSpec(shape, lambda i, spots: (0, 0))

    def moving(size):
        return pl.BlockSpec((tile, size), lambda i, spots: (i, 0))

    def low(*shape):
        return jax.ShapeDtypeStruct(shape, jnp.bfloat16)

    return pl.pallas_call(
        functools.partial(project_kernel, len(pieces)),
        out_shape=(
            low(tokens, features),
            low(tokens, width),
            low(tokens, width),
            low(tokens, width),
            low(features, columns),
        ),
        grid_spec=pltpu.PrefetchScalarGridSpec(
            num_scalar_prefetch=1,
            grid=(tokens // tile,),
            in_specs=[moving(features), still(modulation.shape), still(bias.shape)]
            + [still(piece.shape) for piece in pieces],
            out_specs=(
                moving(features),
                moving(width),
                moving(width),
                moving(width),
                still((features, columns)),
            ),
        ),
        compiler_params=pltpu.CompilerParams(vmem_limit_bytes=48 << 20),
        name="project",
    )(spots, latent, modulation, bias, *pieces)


def project_back_kernel(
    spots, query, key_a, key_b, value_a, value_b, latent, weight,
    grad_a, grad_b, grad_c, grad_d, joined, sums, token_sums,
):
    @pl.when(pl.program_id(0) == 0)
    def _():
        sums[...] = jnp.zeros(sums.shape, jnp.float32)
        token_sums[...] = jnp.zeros(token_sums.shape, jnp.float32)

    flat = jnp.concatenate(
        [
            query[...],
            (key_a[...] + key_b[...].astype(jnp.float32)).astype(jnp.bfloat16),
            (value_a[...] + value_b[...].astype(jnp.float32)).astype(jnp.bfloat16),
        ],
        axis=1,
    )
    joined[...] = flat
    sums[...] += jnp.sum(flat.astype(jnp.float32), axis=0, keepdims=True)
    result = dot(flat, weight[...], ROWS)
    normed = normalise(latent[...].astype(jnp.float32))[0]
    token_sums[0:1, :] += row_sum(result)
    token_sums[1:2, :] += row_sum(result * normed)
    result = result.astype(jnp.bfloat16)
    for k, grad in enumerate((grad_a, grad_b, grad_c, grad_d)):

        @pl.when(pl.program_id(0) == k)
        def _(grad=grad):
            grad[...] = result


def project_back(held_back, spots, query, key_a, key_b, value_a, value_b, latent, weight):
    tokens, width = query.shape
    features, columns = weight.shape
    tile = tokens // 4

    def moving(size):
        return pl.BlockSpec((tile, size), lambda i, spots: (spots[i], 0))

    def still(shape):
        return pl.BlockSpec(shape, lambda i, spots: (0, 0))

    piece = jax.ShapeDtypeStruct((tile, features), jnp.bfloat16)
    return pl.pallas_call(
        after(len(held_back), project_back_kernel),
        out_shape=(
            piece,
            piece,
            piece,
            piece,
            jax.ShapeDtypeStruct((tokens, columns), jnp.bfloat16),
            jax.ShapeDtypeStruct((1, columns), jnp.float32),
            jax.ShapeDtypeStruct((8, features), jnp.float32),
        ),
        grid_spec=pltpu.PrefetchScalarGridSpec(
            num_scalar_prefetch=1,
            grid=(4,),
            in_specs=held(held_back)
            + [moving(width)] * 5 + [moving(features), still(weight.shape)],
            out_specs=(still(piece.shape),) * 4
            + (moving(columns), still((1, columns)), still((8, features))),
        ),
        compiler_params=pltpu.CompilerParams(vmem_limit_bytes=48 << 20),
        name="project_back",
    )(spots, *held_back, query, key_a, key_b, value_a, value_b, latent, weight)


def row_sum(values):
    return jnp.sum(values, axis=0, keepdims=True)


def middle_back_kernel(
    spots, latent, cotangent, branch_one, grad_here, grad_there, modulation, merge,
    middle, middle_grad, branch_one_grad, piece_a, piece_b, piece_c, piece_d, sums,
):
    branch = branch_one[...]
    upstream = cotangent[...].astype(jnp.float32)
    centre = latent[...].astype(jnp.float32) + modulation[2:3, :] * branch
    middle[...] = centre
    normed, scale = normalise(centre)
    grad = grad_here[...].astype(jnp.float32) + grad_there[...].astype(jnp.float32)
    total = upstream + normalise_back(grad * (1.0 + modulation[4:5, :]), normed, scale)
    middle_grad[...] = total
    branch_grad = (modulation[2:3, :] * total).astype(jnp.bfloat16)
    branch_one_grad[...] = branch_grad
    mixed = dot(branch_grad, merge[...], PLAIN).astype(jnp.bfloat16)
    width = piece_a.shape[1]
    for k, piece in enumerate((piece_a, piece_b, piece_c, piece_d)):
        piece[...] = mixed[:, k * width : (k + 1) * width]
    scaled = (modulation[5:6, :] * upstream).astype(jnp.bfloat16).astype(jnp.float32)
    sums[0:1, :] = row_sum(total * branch)
    sums[1:2, :] = row_sum(grad)
    sums[2:3, :] = row_sum(grad * normed)
    sums[3:4, :] = row_sum(branch_grad.astype(jnp.float32))
    sums[4:5, :] = row_sum(scaled)
    sums[5:8, :] = jnp.zeros((3, sums.shape[1]), jnp.float32)


def middle_back(held_back, spots, latent, cotangent, branch_one, here, there, modulation, far, width):
    count, features = here.shape

    def still(shape):
        return pl.BlockSpec(shape, lambda i, spots: (0, 0))

    def picked(place_at):
        return pl.BlockSpec((count, features), lambda i, spots: (spots[place_at], 0))

    def low(*shape):
        return jax.ShapeDtypeStruct(shape, jnp.bfloat16)

    def high(*shape):
        return jax.ShapeDtypeStruct(shape, jnp.float32)

    shapes = (
        high(count, features),
        high(count, features),
        low(count, features),
        low(count, width),
        low(count, width),
        low(count, width),
        low(count, width),
        high(8, features),
    )
    return pl.pallas_call(
        after(len(held_back), middle_back_kernel),
        out_shape=shapes,
        grid_spec=pltpu.PrefetchScalarGridSpec(
            num_scalar_prefetch=1,
            grid=(1,),
            in_specs=held(held_back)
            + [
                picked(0),
                picked(0),
                picked(1),
                still(here.shape),
                still(there.shape),
                still(modulation.shape),
                still((features, features)),
            ],
            out_specs=tuple(still(shape.shape) for shape in shapes),
        ),
        compiler_params=pltpu.CompilerParams(vmem_limit_bytes=48 << 20),
        name="middle_back",
    )(spots, *held_back, latent, cotangent, branch_one, here, there, modulation, far)


def latent_back_kernel(spots, latent, middle_grad, modulation, part_a, part_b, part_c, result):
    normed, scale = normalise(latent[...].astype(jnp.float32))
    grad = (
        part_a[...].astype(jnp.float32)
        + part_b[...].astype(jnp.float32)
        + part_c[...].astype(jnp.float32)
    )
    total = middle_grad[...] + normalise_back(grad * (1.0 + modulation[1:2, :]), normed, scale)
    result[...] = total.astype(jnp.bfloat16)


def latent_back(spots, latent, middle_grad, modulation, parts):
    count, features = middle_grad.shape

    def still(shape):
        return pl.BlockSpec(shape, lambda i, spots: (0, 0))

    square = still((count, features))
    return pl.pallas_call(
        latent_back_kernel,
        out_shape=jax.ShapeDtypeStruct((count, features), jnp.bfloat16),
        grid_spec=pltpu.PrefetchScalarGridSpec(
            num_scalar_prefetch=1,
            grid=(1,),
            in_specs=[
                pl.BlockSpec((count, features), lambda i, spots: (spots[0], 0)),
                square,
                still(modulation.shape),
                square,
                square,
                square,
            ],
            out_specs=square,
        ),
        compiler_params=pltpu.CompilerParams(vmem_limit_bytes=48 << 20),
        name="latent_back",
    )(spots, latent, middle_grad, modulation, *parts)


def modulate_rows(values, offset, scaling):
    return normalise(values)[0] * (1.0 + scaling) + offset


def smooth_gate_both(values):
    cubic = math.sqrt(2.0 / math.pi) * (values + 0.044715 * values * values * values)
    slope = math.sqrt(2.0 / math.pi) * (1.0 + 3.0 * 0.044715 * values * values)
    bend = jnp.tanh(cubic)
    lifted = 0.5 * (1.0 + bend)
    return values * lifted, lifted + 0.5 * values * (1.0 - bend * bend) * slope


def forward_back_kernel(
    steps,
    spot,
    piece_a, piece_b, piece_c, piece_d,
    latent, cotangent, modulation, merge, merge_bias,
    expand_near, expand_far, reduce_near, reduce_far, bias,
    branch_one, normed_two, branch_two_grad, activated, hidden_grad, bias_grad,
    branch_two_here, branch_two_there, grad_here, grad_there,
    forward_sum, backward_sum,
):
    step = pl.program_id(0)

    @pl.when(step == 0)
    def _():
        mixture = jnp.concatenate(
            [piece_a[...], piece_b[...], piece_c[...], piece_d[...]], axis=1
        )
        branch = dot(mixture, merge[...], ROWS) + merge_bias[...].astype(jnp.float32)
        branch_one[...] = branch
        middle = latent[...].astype(jnp.float32) + modulation[2:3, :] * branch
        normed_two[...] = modulate_rows(
            middle, modulation[3:4, :], modulation[4:5, :]
        ).astype(jnp.bfloat16)
        branch_two_grad[...] = (
            modulation[5:6, :] * cotangent[...].astype(jnp.float32)
        ).astype(jnp.bfloat16)
        forward_sum[...] = jnp.zeros(forward_sum.shape, jnp.float32)
        backward_sum[...] = jnp.zeros(backward_sum.shape, jnp.float32)

    def block(expand, reduce):
        hidden = dot(normed_two[...], expand[...], PLAIN) + bias[...].astype(jnp.float32)
        value, slope = smooth_gate_both(hidden)
        value = value.astype(jnp.bfloat16)
        activated[...] = value
        grad = dot(branch_two_grad[...], reduce[...], PLAIN) * slope
        grad = grad.astype(jnp.bfloat16)
        hidden_grad[...] = grad
        bias_grad[...] = jnp.sum(grad.astype(jnp.float32), axis=0, keepdims=True)
        backward_sum[...] += dot(grad, expand[...], ROWS)
        forward_sum[...] += dot(value, reduce[...], ROWS)

    @pl.when(step < steps // 2)
    def _():
        block(expand_near, reduce_near)

    @pl.when(step >= steps // 2)
    def _():
        block(expand_far, reduce_far)

    @pl.when(step == steps - 1)
    def _():
        count = grad_here.shape[0]
        here = pl.ds(pl.multiple_of(spot[1] * count, count), count)
        there = pl.ds(pl.multiple_of((1 - spot[1]) * count, count), count)
        branch_two_here[...] = forward_sum[here, :].astype(jnp.bfloat16)
        branch_two_there[...] = forward_sum[there, :].astype(jnp.bfloat16)
        grad_here[...] = backward_sum[here, :].astype(jnp.bfloat16)
        grad_there[...] = backward_sum[there, :].astype(jnp.bfloat16)


def forward_back(spots, pieces, latent, cotangent, modulation, near, far, merge_bias, bias):
    rows, width = pieces[0].shape
    features = latent.shape[1]
    hidden = bias.shape[1] // 2
    tile = min(512, hidden)
    per = hidden // tile
    steps = 2 * per
    ahead = features // tile

    def still(array):
        return pl.BlockSpec(array.shape, lambda j, spot: (0, 0))

    def picked():
        return pl.BlockSpec((rows, features), lambda j, spot: (spot[0], 0))

    def column(first, lag):
        def place_at(j, spot):
            return (0, first + jnp.clip(j - lag, 0, per - 1))

        return pl.BlockSpec((features, tile), place_at)

    moving = pl.BlockSpec((rows, tile), lambda j, spot: (0, j))
    row_tile = pl.BlockSpec((1, tile), lambda j, spot: (0, j))
    square = pl.BlockSpec((rows, features), lambda j, spot: (0, 0))
    piece = pl.BlockSpec((rows // 2, features), lambda j, spot: (0, 0))
    low = jax.ShapeDtypeStruct((rows, features), jnp.bfloat16)
    high = jax.ShapeDtypeStruct((rows, features), jnp.float32)
    lower = jax.ShapeDtypeStruct((rows // 2, features), jnp.bfloat16)
    return pl.pallas_call(
        functools.partial(forward_back_kernel, steps),
        out_shape=(
            high,
            low,
            low,
            jax.ShapeDtypeStruct((rows, 2 * hidden), jnp.bfloat16),
            jax.ShapeDtypeStruct((rows, 2 * hidden), jnp.bfloat16),
            jax.ShapeDtypeStruct((1, 2 * hidden), jnp.float32),
            lower,
            lower,
            lower,
            lower,
        ),
        grid_spec=pltpu.PrefetchScalarGridSpec(
            num_scalar_prefetch=1,
            grid=(steps,),
            in_specs=[still(piece) for piece in pieces]
            + [
                picked(),
                picked(),
                still(modulation),
                pl.BlockSpec((features, features), lambda j, spot: (0, 0)),
                still(merge_bias),
                column(0, 0),
                column(ahead, per),
                column(per, 0),
                column(ahead + per, per),
                row_tile,
            ],
            out_specs=(square, square, square, moving, moving, row_tile, piece, piece, piece, piece),
            scratch_shapes=[
                pltpu.VMEM((rows, features), jnp.float32),
                pltpu.VMEM((rows, features), jnp.float32),
            ],
        ),
        compiler_params=pltpu.CompilerParams(vmem_limit_bytes=58 << 20),
        name="forward_back",
    )(spots, *pieces, latent, cotangent, modulation, far, merge_bias, near, far, near, far, bias)


def weight_grad_kernel(
    per, waited, first_left, first_right, second_left, second_right, result, turned, turned_second
):
    step = pl.program_id(0)

    @pl.when(step == 0)
    def _():
        turned[...] = first_left[...].T

    @pl.when(step == per)
    def _():
        turned_second[...] = second_left[...].T

    @pl.when(step < per)
    def _():
        result[...] = dot(turned[...], first_right[...], PLAIN).astype(jnp.bfloat16)

    @pl.when(step >= per)
    def _():
        result[...] = dot(turned_second[...], second_right[...], PLAIN).astype(jnp.bfloat16)


def weight_grads(held_back, first_left, first_right, second_left, second_right, tile):
    features = first_left.shape[1]
    per = first_right.shape[1] // tile
    more = second_right.shape[1] // tile

    def still(array):
        return pl.BlockSpec(array.shape, lambda j, spot: (0, 0))

    return pl.pallas_call(
        after(len(held_back), functools.partial(weight_grad_kernel, per)),
        out_shape=jax.ShapeDtypeStruct((features, (per + more) * tile), jnp.bfloat16),
        grid_spec=pltpu.PrefetchScalarGridSpec(
        num_scalar_prefetch=1,
        grid=(per + more,),
        in_specs=held(held_back)
        + [
            still(first_left),
            pl.BlockSpec((first_right.shape[0], tile), lambda j, spot: (0, jnp.minimum(j, per - 1))),
            still(second_left),
            pl.BlockSpec((second_right.shape[0], tile), lambda j, spot: (0, jnp.maximum(j - per, 0))),
        ],
        out_specs=pl.BlockSpec((features, tile), lambda j, spot: (0, j)),
        scratch_shapes=[
            pltpu.VMEM((features, first_left.shape[0]), jnp.bfloat16),
            pltpu.VMEM((features, second_left.shape[0]), jnp.bfloat16),
        ],
        ),
        compiler_params=pltpu.CompilerParams(vmem_limit_bytes=48 << 20),
        name="weight_grads",
    )(jnp.zeros((1,), jnp.int32), *held_back, first_left, first_right, second_left, second_right)


def body(
    sizes,
    latents,
    condition,
    modulation_weight,
    modulation_bias,
    heads_weight,
    heads_bias,
    merge_weight,
    merge_bias,
    expand_weight,
    expand_bias,
    reduce_weight,
    reduce_bias,
    cotangent,
):
    n_shard, n_ctx, n_tp = sizes
    if n_tp != 4 or latents.shape[0] != 1:
        raise ValueError("unsupported split")
    wide = jnp.float32
    narrow = jnp.bfloat16
    owners = ("shard", "ctx")
    row_block = lax.axis_index("shard") * n_ctx + lax.axis_index("ctx")
    tp_index = lax.axis_index("tp")
    pair = tp_index // 2
    side = tp_index % 2
    feature_rows = modulation_weight.shape[0]
    width = modulation_weight.shape[2]
    hidden_width = expand_weight.shape[1]
    latent = latents[0]
    tokens, features = latent.shape
    group = tokens // 2
    count = tokens // n_tp

    def once(values, token):
        return values + token.astype(values.dtype)

    conditions = gather_small(condition[0], "shard", n_shard)
    started = blank_after(conditions)
    heads_flat = once(heads_weight.reshape(feature_rows, 3 * width), started)
    if n_shard > 8 or n_ctx != 2:
        heads_rows = None
    else:
        heads_rows = swapped(heads_flat, "shard", n_shard)
    far = swap(
        jnp.concatenate([merge_weight, expand_weight, reduce_weight], axis=1), "tp", n_tp, 2
    )
    merge_started = once(merge_weight, started)
    merge_near = swap(merge_started, "tp", n_tp, 1)
    merge_last = swap(merge_started, "tp", n_tp, 3)
    near_full = lax.all_gather(
        jnp.concatenate([expand_weight, reduce_weight], axis=1), owners, axis=0, tiled=True
    )
    silu_rows = jax.nn.silu(
        lax.dynamic_slice_in_dim(conditions, row_block * feature_rows, feature_rows, 1).astype(wide)
    ).astype(narrow)
    partial = product("ld,dkf->lkf", silu_rows, modulation_weight)
    local_modulation = scatter_small(partial, "shard", n_shard)
    local_modulation = add_all(local_modulation, "ctx", n_ctx) + modulation_bias.astype(wide)
    bias_away = swap(expand_bias, "tp", n_tp, 2)
    for early in [bias_away] + (heads_rows or [])[1:]:
        local_modulation = local_modulation + blank_after(early)
    modulation = gather_small(local_modulation, "tp", n_tp)
    modulation = jnp.swapaxes(modulation, 0, 1).reshape(6, features)
    offset_one, scaling_one, gate_one, offset_two, scaling_two, gate_two = (
        modulation[k][None] for k in range(6)
    )
    issued = blank_after(local_modulation)
    far_rows = jnp.concatenate(
        [merge_weight, merge_near, far[:, :width], merge_last, far[:, width:]], axis=1
    )
    far_full = lax.all_gather(
        far_rows + issued.astype(narrow), owners, axis=0, tiled=True
    )
    if heads_rows is None:
        heads_pieces = [lax.all_gather(heads_flat, owners, axis=0, tiled=True)]
        spots = jnp.zeros((1,), jnp.int32)
    else:
        shard = lax.axis_index("shard")
        ctx = lax.axis_index("ctx")
        heads_other = [swap(once(rows, issued), "ctx", n_ctx, 1) for rows in heads_rows]
        heads_pieces = heads_rows + heads_other
        places = [(shard ^ k) * n_ctx for k in range(n_shard)]
        spots = jnp.stack([p + ctx for p in places] + [p + 1 - ctx for p in places])
    expand_biases = jnp.concatenate([expand_bias, bias_away])[None]

    bias_rows = heads_bias.astype(wide)
    project_bias = jnp.concatenate([bias_rows[0], jnp.zeros_like(bias_rows[0]), bias_rows[1]])
    normed_one, queries, keys_here, values_here, heads_full = project(
        spots, latent, modulation, project_bias[None], heads_pieces
    )
    keys = (keys_here, swap(keys_here, "ctx", n_ctx, 1))
    values = (values_here, swap(values_here, "ctx", n_ctx, 1))

    mixed_away, *kept_away = attend(1 - pair, group, queries, keys, values)
    mixed_near, *kept_near = attend(pair, group, queries, keys, values)
    across = swap(mixed_away, "tp", n_tp, 2)
    pieces = [mixed_near, swap(mixed_near, "tp", n_tp, 1), across, swap(across, "tp", n_tp, 1)]
    (
        branch_one,
        normed_two,
        branch_two_grad,
        activated,
        hidden_grad,
        hidden_bias_grad,
        branch_two_here,
        branch_two_there,
        grad_here,
        grad_there,
    ) = forward_back(
        jnp.stack([pair, side]),
        pieces,
        latent,
        cotangent[0],
        modulation,
        near_full,
        far_full,
        merge_bias[None],
        expand_biases,
    )
    arrived = swap(grad_there, "tp", n_tp, 1)
    hidden_grads = weight_grads(
        [], branch_two_grad, activated, normed_two, hidden_grad, min(512, hidden_width)
    )
    middle, middle_grad, branch_one_grad, *mixture_grads, second_sums = middle_back(
        [hidden_grads],
        jnp.stack([tp_index, side]),
        latent,
        cotangent[0],
        branch_one,
        grad_here,
        arrived,
        modulation,
        far_full,
        width,
    )
    received = [
        swap(mixture_grads[k], "tp", n_tp, k) if k else mixture_grads[0] for k in range(n_tp)
    ]
    scattered = lax.psum_scatter(
        hidden_grads,
        owners,
        scatter_dimension=0,
        tiled=True,
    )

    arrived_two = swap(branch_two_there, "tp", n_tp, 1)
    branch_two = (
        branch_two_here.astype(wide)
        + arrived_two.astype(wide)
        + reduce_bias.astype(wide)
    )
    own_output = (middle + gate_two * branch_two).astype(narrow)
    output_pieces = spread(own_output)
    output = assembled(output_pieces)
    gate_two_grad = jnp.sum(
        block_of(cotangent[0], tp_index, count).astype(wide) * branch_two, axis=0, keepdims=True
    )

    query_grad, key_grad_a, key_grad_b, value_grad_a, value_grad_b = attend_back(
        jnp.stack([pair, tp_index]), queries, received, kept_near, kept_away, keys, values
    )
    here, by_one, by_two, by_three, projected_grad, projected_sums, first_sums = project_back(
        output_pieces[1:3],
        jnp.stack([tp_index ^ k for k in range(n_tp)]),
        query_grad,
        key_grad_a,
        swap(key_grad_b, "ctx", n_ctx, 1),
        value_grad_a,
        swap(value_grad_b, "ctx", n_ctx, 1),
        latent,
        heads_full,
    )
    heads_bias_grad = jnp.concatenate(
        [projected_sums[0, :width], projected_sums[0, 2 * width :]]
    )
    beside = swap(by_three, "tp", n_tp, 1)
    from_far = [
        swap((by_two.astype(wide) + beside.astype(wide)).astype(narrow), "tp", n_tp, 2)
    ]
    near_sum = swap(once(by_one, blank_after(beside)), "tp", n_tp, 1)
    own_mixture = jnp.concatenate([block_of(piece, side, count) for piece in pieces], axis=1)
    scattered_more = lax.psum_scatter(
        weight_grads(
            [scattered, beside], normed_one, projected_grad, branch_one_grad, own_mixture, width),
        owners,
        scatter_dimension=0,
        tiled=True,
    )
    heads_weight_grad = scattered_more[:, : 3 * width].astype(wide)
    merge_pieces = scattered_more[:, 3 * width :]
    reduce_near, reduce_far, expand_near, expand_far = (
        scattered[:, k * hidden_width : (k + 1) * hidden_width] for k in range(4)
    )
    far_pair = jnp.concatenate([reduce_far, expand_far], axis=1)
    both = swap(far_pair, "tp", n_tp, 2).astype(wide)
    reduce_weight_grad = reduce_near.astype(wide) + both[:, :hidden_width]
    expand_weight_grad = expand_near.astype(wide) + both[:, hidden_width:]
    merge_weight_grad = merge_pieces[:, :width].astype(wide)
    for k in range(1, n_tp):
        merge_weight_grad = merge_weight_grad + swap(
            merge_pieces[:, k * width : (k + 1) * width], "tp", n_tp, k
        ).astype(wide)
    expand_bias_grad = hidden_bias_grad[0, :hidden_width] + swap(
        hidden_bias_grad[0, hidden_width:], "tp", n_tp, 2
    )
    sums = jnp.concatenate([second_sums[:3], gate_two_grad, second_sums[3:5]], axis=0)
    first_sums = first_sums[:2]

    own_grad = latent_back(
        tp_index[None],
        latent,
        middle_grad,
        modulation,
        (here, near_sum, *from_far),
    )
    latent_pieces = spread(own_grad)
    vectors = jnp.concatenate([first_sums, sums], axis=0)
    vectors = vectors + blank_after(latent_pieces[1]) + blank_after(latent_pieces[2])
    vectors = vectors + blank_after(both)
    vectors = add_all(vectors, "tp", n_tp)
    local_grad = lax.dynamic_slice_in_dim(vectors[:6], tp_index * width, width, 1)
    common = jnp.concatenate(
        [
            local_grad.reshape(-1),
            vectors[6],
            vectors[7],
            expand_bias_grad,
            heads_bias_grad,
        ]
    )
    common = add_all(common, "ctx", n_ctx)
    local_grad = common[: 6 * width].reshape(6, width)
    biases = add_all(common[6 * width :], "shard", n_shard)
    modulation_grad = gather_small(local_grad, "shard", n_shard)
    modulation_bias_grad = jnp.sum(modulation_grad, axis=0)
    modulation_weight_grad = jnp.einsum(
        "ld,lkf->dkf", silu_rows.astype(wide), modulation_grad, precision=lax.Precision.HIGHEST
    )
    latents_grad = assembled(latent_pieces).astype(wide)
    cuts = [features, features, hidden_width, 2 * width]
    edges = [sum(cuts[:k]) for k in range(len(cuts) + 1)]
    merge_bias_grad, reduce_bias_grad, expand_bias_grad, heads_bias_grad = (
        biases[edges[k] : edges[k + 1]] for k in range(4)
    )
    return (
        output[None],
        latents_grad[None],
        modulation_weight_grad,
        modulation_bias_grad,
        heads_weight_grad.reshape(feature_rows, 3, width),
        heads_bias_grad.reshape(2, width),
        merge_weight_grad,
        merge_bias_grad,
        expand_weight_grad,
        expand_bias_grad,
        reduce_weight_grad,
        reduce_bias_grad,
    )


def solution(mesh):
    sizes = tuple(mesh.shape[name] for name in ("shard", "ctx", "tp"))
    return jax.shard_map(
        functools.partial(body, sizes),
        mesh=mesh,
        in_specs=(
            P("shard", "ctx", None),
            P("shard", None),
            P(("shard", "ctx"), None, "tp"),
            P(None, "tp"),
            P(("shard", "ctx"), None, "tp"),
            P(None, "tp"),
            P(("shard", "ctx"), "tp"),
            P(),
            P(("shard", "ctx"), "tp"),
            P("tp"),
            P(("shard", "ctx"), "tp"),
            P(),
            P("shard", "ctx", None),
        ),
        out_specs=(
            P("shard", "ctx", None),
            P("shard", "ctx", None),
            P(("shard", "ctx"), None, "tp"),
            P(None, "tp"),
            P(("shard", "ctx"), None, "tp"),
            P(None, "tp"),
            P(("shard", "ctx"), "tp"),
            P(),
            P(("shard", "ctx"), "tp"),
            P("tp"),
            P(("shard", "ctx"), "tp"),
            P(),
        ),
        check_vma=False,
    )
```
